32 devices in a mesh: dp: 8 (over y, x, core), mp: 4 (over z).
Axes of the slice: x: 2, y: 2, z: 4, core: 2. Of those that a mesh axis runs over, the one named last changes fastest.
Arguments:
- patches: bfloat16 [192, 196, 768], P('dp'), may hold values from -6 to 6
- counts: int32 [192], P('dp'), may hold values from 39 to 98, as said below
- kept_patches: int32 [192, 128], P('dp'), may hold values from 0 to 195, as said below
- cotangent: bfloat16 [192, 128, 768], P('dp'), may hold values from -6 to 6
- norm_gains: bfloat16 [2, 768], P(None, 'dp'), may hold values from 0.099609375 to 1.8984375
- shifts: bfloat16 [4, 768], P(None, 'dp'), may hold values from -3 to 3
- qkv_weight: bfloat16 [768, 3, 768], P('dp', None, 'mp'), may hold values from -0.21875 to 0.21875
- qkv_bias: bfloat16 [2, 768], P(None, 'mp'), may hold values from -3 to 3
- proj_weight: bfloat16 [768, 768], P('mp', 'dp'), may hold values from -0.625 to 0.625
- fc1_weight: bfloat16 [768, 3072], P('dp', 'mp'), may hold values from -0.21875 to 0.21875
- fc1_bias: bfloat16 [3072], P('mp'), may hold values from -3 to 3
- fc2_weight: bfloat16 [3072, 768], P('mp', 'dp'), may hold values from -0.109375 to 0.109375
Outputs:
- block_out: bfloat16 [192, 128, 768], P('dp')
- patch_grad: float32 [192, 196, 768], P('dp')
- gain_grad: float32 [2, 768], P(None, 'dp')
- shift_grad: float32 [4, 768], P(None, 'dp')
- qkv_grad: float32 [768, 3, 768], P('dp', None, 'mp')
- qkv_bias_grad: float32 [2, 768], P(None, 'mp')
- proj_grad: float32 [768, 768], P('mp', 'dp')
- fc1_grad: float32 [768, 3072], P('dp', 'mp')
- fc1_bias_grad: float32 [3072], P('mp')
- fc2_grad: float32 [3072, 768], P('mp', 'dp')
The draws below stay inside these ranges and needn't reach their ends.
Inputs may be any that keep to these rules, and one draw needn't show every extreme that they name: `counts`: some image has exactly 98 visible patches and some exactly 39. `kept_patches`: each image's row holds 128 distinct patch numbers; its first counts[i] are the visible patches.
All inputs are finite; a program needn't handle non-finite values.
Results may differ from the reference program's by a relative error of at most 0.02.
Values may be sent and summed in bfloat16 or wider, within the bound.
A program may use at most 192 MiB of HBM per device.

```python
import math
import jax
import jax.numpy as jnp
from jax import lax

D = 768
HEADS = 12
HD = 64
FF = 3072
PATCHES = 196
SLOT = 128
KEEP_MIN = 39
KEEP_MAX = 98
INNER = 768
IMAGES = 192
N_MP = 4


def draw_counts(key, part):
    first_key, second_key, third_key = jax.random.split(key, 3)
    values = jax.random.randint(first_key, (IMAGES,), KEEP_MIN, KEEP_MAX + 1)
    top_place = jax.random.randint(second_key, (), 0, IMAGES)
    least_place = (top_place + 1 + jax.random.randint(third_key, (), 0, IMAGES - 1)) % IMAGES
    values = values.at[least_place].set(KEEP_MIN)
    values = values.at[top_place].set(KEEP_MAX)
    return values.astype(jnp.int32)


def draw_kept_patches(key, part):
    image_keys = jax.random.split(key, IMAGES)
    orders = jax.vmap(lambda one_key: jax.random.permutation(one_key, PATCHES))(image_keys)
    return orders[:, :SLOT].astype(jnp.int32)


def level_of(stream_key, dims, cuts, low, largest):
    level, own = 1.0, jax.random.fold_in(stream_key, 6)
    for axis_at, shards_of in cuts:
        heights = jnp.exp(jax.random.uniform(jax.random.fold_in(own, axis_at), (shards_of,), jnp.float32, low / len(cuts), largest / len(cuts)))
        level = level * jnp.repeat(heights, dims[axis_at] // shards_of).reshape([-1 if axis == axis_at else 1 for axis in range(len(dims))])
    return level


def scatter_about(rng, dims, spread, reach, shards=(), dtype=jnp.bfloat16):
    values = spread * jax.random.normal(rng, dims, jnp.float32)
    if shards:
        values = values * level_of(rng, dims, shards, -0.22, 0.18)
    return jnp.clip(values, -reach, reach).astype(dtype)


def setup_inputs(seed: int = 0) -> dict:
    keys = jax.random.split(jax.random.key(seed), 13)
    return {
        "patches": scatter_about(keys[0], (IMAGES, PATCHES, D), 1.0, 6.0, ((0, 8),)),
        "counts": draw_counts(jax.random.fold_in(keys[12], 71), 0),
        "kept_patches": draw_kept_patches(jax.random.fold_in(keys[12], 71), 0),
        "cotangent": scatter_about(keys[3], (IMAGES, SLOT, D), 1.0, 6.0, ((0, 8),)),
        "norm_gains": jnp.clip(1.0 + 0.18 * jax.random.normal(keys[4], (2, D), jnp.float32), 0.099609375, 1.8984375).astype(jnp.bfloat16),
        "shifts": scatter_about(keys[5], (4, D), 0.5, 3.0, ((1, 8),)),
        "qkv_weight": scatter_about(keys[6], (D, 3, INNER), D ** -0.5, 0.21875, ((0, 8), (2, 4))),
        "qkv_bias": scatter_about(keys[7], (2, INNER), 0.5, 3.0, ((1, 4),)),
        "proj_weight": scatter_about(keys[8], (INNER, D), (D // 8) ** -0.5, 0.625, ((0, 4), (1, 8))),
        "fc1_weight": scatter_about(keys[9], (D, FF), D ** -0.5, 0.21875, ((0, 8), (1, 4))),
        "fc1_bias": scatter_about(keys[10], (FF,), 0.5, 3.0, ((0, 4),)),
        "fc2_weight": scatter_about(keys[11], (FF, D), FF ** -0.5, 0.109375, ((0, 4), (1, 8))),
    }


@jax.custom_vjp
def low(v):
    return lax.optimization_barrier(v.astype(jnp.bfloat16)).astype(jnp.float32)

@jax.custom_vjp
def low_back(v):
    return v

def low_keep(v):
    return (low(v), None)

def low_pass(kept, grad):
    return (grad,)

def back_keep(v):
    return (v, None)

def back_low(kept, grad):
    return (low(grad),)
low.defvjp(low_keep, low_pass)
low_back.defvjp(back_keep, back_low)
epsilon = 1e-06
highest = lax.Precision.HIGHEST

def layer_norm(values, gain_row, shift_row):
    row_mean = lax.optimization_barrier(jnp.mean(values, axis=-1, keepdims=True))
    centred = values - row_mean
    variance = lax.optimization_barrier(jnp.mean(centred * centred, axis=-1, keepdims=True))
    return centred * lax.rsqrt(variance + epsilon) * gain_row + shift_row

def project(left, right):
    return jnp.einsum('isd,dc->isc', left, right, precision=highest)

def forward(patch_block, count_block, kept_block, params):
    norm_gains, shifts, qkv_weight, qkv_bias, proj_weight, fc1_weight, fc1_bias, fc2_weight = params
    visible = jax.vmap(lambda one_image, one_index: one_image[one_index])(patch_block, kept_block)
    images = visible.shape[0]
    key_live = jnp.arange(SLOT)[None, :] < count_block[:, None]
    heads_group = HEADS // N_MP
    group_width = heads_group * HD
    hidden_width = FF // N_MP
    score_scale = HD ** (-0.5)
    normed_in = low(layer_norm(visible, norm_gains[0], shifts[0]))
    attention = jnp.zeros_like(visible)
    for group_index in range(N_MP):
        column_start = group_index * group_width
        column_end = column_start + group_width
        source = low_back(normed_in)
        queries = low(low_back(project(source, qkv_weight[:, 0, column_start:column_end]) + qkv_bias[0, column_start:column_end]))
        key_rows = low(low_back(project(source, qkv_weight[:, 1, column_start:column_end])))
        value_rows = low(low_back(project(source, qkv_weight[:, 2, column_start:column_end]) + qkv_bias[1, column_start:column_end]))
        queries = queries.reshape(images, SLOT, heads_group, HD)
        key_rows = key_rows.reshape(images, SLOT, heads_group, HD)
        value_rows = value_rows.reshape(images, SLOT, heads_group, HD)
        scores = low_back(jnp.einsum('iqhe,ikhe->ihqk', queries, key_rows, precision=highest) * score_scale)
        scores = jnp.where(key_live[:, None, None, :], scores, -1e+30)
        probability = low(jax.nn.softmax(scores, axis=-1))
        attended = jnp.einsum('ihqk,ikhe->iqhe', probability, value_rows, precision=highest)
        attended = low(low_back(attended.reshape(images, SLOT, group_width)))
        attention = attention + low(project(attended, proj_weight[column_start:column_end, :]))
    middle = visible + low_back(attention + shifts[1])
    normed_mid = low(layer_norm(middle, norm_gains[1], shifts[2]))
    mlp_branch = jnp.zeros_like(middle)
    for group_index in range(N_MP):
        column_start = group_index * hidden_width
        column_end = column_start + hidden_width
        source = low_back(normed_mid)
        hidden_pre = low_back(project(source, fc1_weight[:, column_start:column_end]) + fc1_bias[column_start:column_end])
        hidden_act = low(jax.nn.gelu(hidden_pre, approximate=False))
        mlp_branch = mlp_branch + low(project(hidden_act, fc2_weight[column_start:column_end, :]))
    return middle + low_back(mlp_branch + shifts[3])

def reference(patches, counts, kept_patches, cotangent, norm_gains, shifts, qkv_weight, qkv_bias, proj_weight, fc1_weight, fc1_bias, fc2_weight):
    params = tuple((weight_item.astype(jnp.float32) for weight_item in (norm_gains, shifts, qkv_weight, qkv_bias, proj_weight, fc1_weight, fc1_bias, fc2_weight)))
    block_size = math.gcd(IMAGES, 32)
    blocks = IMAGES // block_size

    def split_blocks(array):
        return array.reshape((blocks, block_size) + array.shape[1:])

    def one_block(totals, block_items):
        patch_block, count_block, kept_block, cot_block = block_items
        live_rows = (jnp.arange(SLOT)[None, :] < count_block[:, None])[:, :, None]

        def run_block(patch_values, weights):
            return forward(patch_values, count_block, kept_block, weights)
        outputs, pullback = jax.vjp(run_block, patch_block.astype(jnp.float32), params)
        seed_grad = jnp.where(live_rows, cot_block.astype(jnp.float32), 0.0)
        patch_grad, weight_grads = pullback(seed_grad)
        totals = tuple((total_item + grad_item for total_item, grad_item in zip(totals, weight_grads)))
        block_out = jnp.where(live_rows, outputs, 0.0).astype(jnp.bfloat16)
        return (totals, (block_out, patch_grad))
    start_totals = tuple((jnp.zeros_like(weight_item) for weight_item in params))
    totals, (block_out, patch_grad) = lax.scan(one_block, start_totals, (split_blocks(patches), split_blocks(counts), split_blocks(kept_patches), split_blocks(cotangent)))
    gain_grad, shift_grad, qkv_grad, qkv_bias_grad, proj_grad, fc1_grad, fc1_bias_grad, fc2_grad = totals
    return (block_out.reshape(IMAGES, SLOT, D), patch_grad.reshape(IMAGES, PATCHES, D), gain_grad, shift_grad, qkv_grad, qkv_bias_grad, proj_grad, fc1_grad, fc1_bias_grad, fc2_grad)
```

```python
import jax
import jax.numpy as jnp
from jax import lax
from jax.sharding import PartitionSpec as P

HD = 64
KEEP_MAX = 98
CHUNK = 12

epsilon = 1e-06
f32 = jnp.float32
bf16 = jnp.bfloat16


def norm_forward(values, gain_row, shift_row):
    row_mean = jnp.mean(values, axis=-1, keepdims=True)
    centred = values - row_mean
    inverse = lax.rsqrt(jnp.mean(centred * centred, axis=-1, keepdims=True) + epsilon)
    normed = centred * inverse
    return (normed * gain_row + shift_row, normed, inverse)


def norm_backward(grad_normed, normed, inverse, gain_row):
    scaled = grad_normed * gain_row
    first_mean = jnp.mean(scaled, axis=-1, keepdims=True)
    second_mean = jnp.mean(scaled * normed, axis=-1, keepdims=True)
    grad_input = inverse * (scaled - first_mean - normed * second_mean)
    return (grad_input, jnp.sum(grad_normed * normed, axis=0), jnp.sum(grad_normed, axis=0))


def gelu_exact(values):
    return jax.nn.gelu(values, approximate=False)


def dot(left, right, dims, out=f32):
    return lax.dot_general(left, right, (dims, ((), ())), preferred_element_type=out)


def per_device(
    patches,
    counts,
    kept_patches,
    cotangent,
    norm_gains,
    shifts,
    qkv_weight,
    qkv_bias,
    proj_weight,
    fc1_weight,
    fc1_bias,
    fc2_weight,
):
    image_count, patch_count, width = patches.shape
    slot_count = kept_patches.shape[1]
    rows_used = min(slot_count, -(-KEEP_MAX // 8) * 8)
    n_mp = lax.axis_size("mp")
    me = lax.axis_index("mp")
    group_width = qkv_weight.shape[2]
    inner = group_width * n_mp
    heads = inner // HD
    hidden_here = fc1_weight.shape[1]
    hidden = hidden_here * n_mp
    scale = HD ** (-0.5)

    gain = lax.all_gather(norm_gains, "dp", axis=1, tiled=True).astype(f32)
    shift = lax.all_gather(shifts, "dp", axis=1, tiled=True).astype(f32)
    qkv = lax.all_gather(lax.all_gather(qkv_weight, "mp", axis=2, tiled=True), "dp", axis=0, tiled=True)
    qkv = qkv.reshape(width, 3 * inner)
    qkv_b = lax.all_gather(qkv_bias, "mp", axis=1, tiled=True).astype(f32)
    proj = lax.all_gather(lax.all_gather(proj_weight.T, "mp", axis=1, tiled=True), "dp", axis=0, tiled=True)
    fc1 = lax.all_gather(lax.all_gather(fc1_weight, "mp", axis=1, tiled=True), "dp", axis=0, tiled=True)
    fc1_b = lax.all_gather(fc1_bias, "mp", axis=0, tiled=True).astype(f32)
    fc2 = lax.all_gather(lax.all_gather(fc2_weight.T, "mp", axis=1, tiled=True), "dp", axis=0, tiled=True)

    chunk = CHUNK if image_count % CHUNK == 0 else 1
    totals = None
    outs, pgs = [], []
    for first in range(0, image_count, chunk):
        n = chunk
        tokens = n * rows_used
        kept = kept_patches[first : first + n, :rows_used]
        count = counts[first : first + n]
        live = lax.broadcasted_iota(jnp.int32, (n, rows_used), 1) < count[:, None]
        live_rows = live.reshape(tokens, 1)
        key_live = live[:, None, None, :]
        onehot = (kept[:, :, None] == lax.broadcasted_iota(jnp.int32, (1, 1, patch_count), 2)).astype(bf16)
        visible = jnp.einsum("irp,ipd->ird", onehot, patches[first : first + n], preferred_element_type=f32)
        visible = visible.reshape(tokens, width)
        normed_in, plain_in, inv_in = norm_forward(visible, gain[0], shift[0])
        source_in = normed_in.astype(bf16)
        projected = dot(source_in, qkv, ((1,), (0,)))
        hs = (n, rows_used, heads, HD)
        q = (projected[:, :inner] + qkv_b[0]).astype(bf16).reshape(hs)
        k = projected[:, inner : 2 * inner].astype(bf16).reshape(hs)
        v = (projected[:, 2 * inner :] + qkv_b[1]).astype(bf16).reshape(hs)
        scores = jnp.einsum("iqhe,ikhe->ihqk", q, k, preferred_element_type=f32) * scale
        scores = jnp.where(key_live, scores, -1e30)
        mx = jnp.max(scores, axis=-1, keepdims=True)
        ex = jnp.exp(scores - mx)
        prob = ex / jnp.sum(ex, axis=-1, keepdims=True)
        prob_low = prob.astype(bf16)
        attended = jnp.einsum("ihqk,ikhe->iqhe", prob_low, v, preferred_element_type=f32)
        attended = attended.reshape(tokens, inner).astype(bf16)
        attention = dot(attended, proj, ((1,), (1,))) + shift[1]
        middle = visible + attention
        normed_mid, plain_mid, inv_mid = norm_forward(middle, gain[1], shift[2])
        source_mid = normed_mid.astype(bf16)
        hidden_pre = dot(source_mid, fc1, ((1,), (0,))) + fc1_b
        hidden_float, pull = jax.vjp(gelu_exact, hidden_pre)
        hidden_act = hidden_float.astype(bf16)
        mlp = dot(hidden_act, fc2, ((1,), (1,))) + shift[3]
        block_out = jnp.where(live_rows, middle + mlp, 0.0).astype(bf16)
        outs.append(jnp.pad(block_out.reshape(n, rows_used, width), ((0, 0), (0, slot_count - rows_used), (0, 0))))
        cot = cotangent[first : first + n, :rows_used].reshape(tokens, width)
        grad_mlp = jnp.where(live_rows, cot, jnp.zeros_like(cot))
        grad_out = grad_mlp.astype(f32)
        grad_act = dot(grad_mlp, fc2, ((1,), (0,)))
        grad_pre = pull(grad_act)[0].astype(bf16)
        act_here = lax.dynamic_slice_in_dim(hidden_act, me * hidden_here, hidden_here, 1)
        pre_here = lax.dynamic_slice_in_dim(grad_pre, me * hidden_here, hidden_here, 1)
        g_fc2 = dot(grad_mlp, act_here, ((0,), (0,)))
        g_fc1 = dot(source_mid, pre_here, ((0,), (0,)))
        g_fc1b = jnp.sum(pre_here.astype(f32), axis=0)
        gnm = dot(grad_pre, fc1, ((1,), (1,)))
        gfm, gain_mid, shift_mid = norm_backward(gnm, plain_mid, inv_mid, gain[1])
        grad_middle = grad_out + gfm
        ga = grad_middle.astype(bf16)
        att_here = lax.dynamic_slice_in_dim(attended, me * group_width, group_width, 1)
        g_proj = dot(ga, att_here, ((0,), (0,)))
        gat = dot(ga, proj, ((1,), (0,))).astype(bf16).reshape(hs)
        gp = jnp.einsum("iqhe,ikhe->ihqk", gat, v, preferred_element_type=f32)
        delta = jnp.sum(prob * gp, axis=-1, keepdims=True)
        gs = (prob * (gp - delta)).astype(bf16)
        gq = (jnp.einsum("ihqk,ikhe->iqhe", gs, k, preferred_element_type=f32) * scale).astype(bf16)
        gk = (jnp.einsum("ihqk,iqhe->ikhe", gs, q, preferred_element_type=f32) * scale).astype(bf16)
        gv = jnp.einsum("ihqk,iqhe->ikhe", prob_low, gat, preferred_element_type=f32).astype(bf16)
        gq, gk, gv = (t.reshape(tokens, inner) for t in (gq, gk, gv))
        gqh, gkh, gvh = (
            lax.dynamic_slice_in_dim(t, me * group_width, group_width, 1) for t in (gq, gk, gv)
        )
        g_qkv = dot(source_in, jnp.concatenate([gqh, gkh, gvh], axis=1), ((0,), (0,)))
        g_qb = jnp.stack([jnp.sum(gqh.astype(f32), axis=0), jnp.sum(gvh.astype(f32), axis=0)])
        gni = dot(jnp.concatenate([gq, gk, gv], axis=1), qkv, ((1,), (1,)))
        gfi, gain_in, shift_in = norm_backward(gni, plain_in, inv_in, gain[0])
        grad_visible = grad_middle + gfi
        pgs.append(
            jnp.einsum(
                "irp,ird->ipd",
                onehot,
                grad_visible.reshape(n, rows_used, width).astype(bf16),
                preferred_element_type=f32,
            )
        )
        small = jnp.stack(
            [
                gain_in,
                gain_mid,
                shift_in,
                jnp.sum(ga.astype(f32), axis=0),
                shift_mid,
                jnp.sum(grad_out, axis=0),
            ]
        )
        parts = (small, g_qkv, g_proj, g_fc1, g_fc2, g_qb, g_fc1b)
        totals = parts if totals is None else tuple(a + b for a, b in zip(totals, parts))
    small, g_qkv, g_proj, g_fc1, g_fc2, g_qb, g_fc1b = totals
    big = jnp.concatenate([g_qkv, g_proj, g_fc1, g_fc2], axis=1).astype(bf16)
    big = lax.psum_scatter(big, "dp", scatter_dimension=0, tiled=True).astype(f32)
    a, b, c = 3 * group_width, 4 * group_width, 4 * group_width + hidden_here
    small = lax.psum_scatter(small, "dp", scatter_dimension=1, tiled=True)
    g_qb, g_fc1b = lax.psum((g_qb, g_fc1b), "dp")
    return (
        jnp.concatenate(outs, axis=0),
        jnp.concatenate(pgs, axis=0),
        small[:2],
        small[2:],
        big[:, :a].reshape(-1, 3, group_width),
        g_qb,
        big[:, a:b].T,
        big[:, b:c],
        g_fc1b,
        big[:, c:].T,
    )


def solution(mesh):
    placed = (
        P("dp", None, None),
        P("dp"),
        P("dp", None),
        P("dp", None, None),
        P(None, "dp"),
        P(None, "dp"),
        P("dp", None, "mp"),
        P(None, "mp"),
        P("mp", "dp"),
        P("dp", "mp"),
        P("mp"),
        P("mp", "dp"),
    )
    return jax.shard_map(
        per_device,
        mesh=mesh,
        in_specs=placed,
        out_specs=(
            P("dp", None, None),
            P("dp", None, None),
            P(None, "dp"),
            P(None, "dp"),
            P("dp", None, "mp"),
            P(None, "mp"),
            P("mp", "dp"),
            P("dp", "mp"),
            P("mp"),
            P("mp", "dp"),
        ),
        check_vma=False,
    )
```

```python
import functools

import jax
import jax.numpy as jnp
from jax import lax
from jax.experimental import pallas as pl
from jax.experimental.pallas import tpu as pltpu
from jax.sharding import PartitionSpec as P

HD = 64
KEEP_MAX = 98
ROWS = 112
KEYS = 128
BLOCK = 256
GROUP_MAX = 24
EPSILON = 1e-06
VMEM_BYTES = 59 * 2**20

f32 = jnp.float32
bf16 = jnp.bfloat16

NN = (((1,), (0,)), ((), ()))
NT = (((1,), (1,)), ((), ()))
TN = (((0,), (0,)), ((), ()))


def dot(left, right, dims=NN):
    return lax.dot_general(left, right, dims, preferred_element_type=f32)


def norm_stats(values):
    row_mean = jnp.mean(values, axis=-1, keepdims=True)
    centred = values - row_mean
    inverse = lax.rsqrt(jnp.mean(centred * centred, axis=-1, keepdims=True) + EPSILON)
    return centred * inverse, inverse


def norm_pull(grad_normed, normed, inverse, gain_row):
    scaled = grad_normed * gain_row
    first_mean = jnp.mean(scaled, axis=-1, keepdims=True)
    second_mean = jnp.mean(scaled * normed, axis=-1, keepdims=True)
    return inverse * (scaled - first_mean - normed * second_mean)


def fold_rows(values):
    rows, width = values.shape
    return jnp.sum(values.reshape(rows // 8, 8, width), axis=0)


def gelu_parts(u):
    bell = jnp.exp(u * u * -0.5)
    t = 1.0 / (1.0 + 0.23164190 * jnp.abs(u))
    poly = 0.5307027145
    for c in (-0.7265760135, 0.7107068705, -0.142248368, 0.127414796):
        poly = poly * t + c
    tail = poly * t * bell
    cdf = jnp.where(u >= 0, 1.0 - tail, tail)
    return u * cdf, cdf + u * bell * 0.3989422804014327


def fill_offsets(counts, offs, images):
    def step(i, total):
        offs[i] = total
        return total + lax.div(counts[i] + 15, 16) * 16

    return lax.fori_loop(0, images, step, 0)


def block_count(offs, images):
    return lax.div(offs[images - 1] + KEYS + BLOCK - 1, BLOCK)


def lane_split(values):
    left = lax.broadcasted_iota(jnp.int32, values.shape, 1) < HD
    zero = jnp.zeros_like(values)
    return jnp.concatenate([jnp.where(left, values, zero), jnp.where(left, zero, values)], axis=0)


def row_block(b):
    return pl.ds(pl.multiple_of(b * BLOCK, BLOCK), BLOCK)


def attend_kernel(
    images, pairs, counts, kept, patches, cot, wqkv, wproj, vec, bias,
    vis_o, gm_o, qkv_o, att_o, prob_o, mid_o,
    offs, pbuf, cbuf, vis, gm, qkv, att, prob, mid, in_sem, cot_sem, blk_sem, prob_sem,
):
    width = vis.shape[1]
    inner = att.shape[1]
    fill_offsets(counts, offs, images)
    nblk = block_count(offs, images)

    def patch_copy(i):
        return pltpu.make_async_copy(patches.at[i], pbuf.at[i], in_sem.at[i])

    def cot_copy(i):
        return pltpu.make_async_copy(cot.at[i, pl.ds(0, ROWS)], cbuf.at[i], cot_sem.at[i])

    def start_in(i, carry):
        patch_copy(i).start()
        cot_copy(i).start()
        return carry

    lax.fori_loop(0, images, start_in, 0)

    def clear(b, carry):
        rows = row_block(b)
        vis[rows, :] = jnp.zeros((BLOCK, width), bf16)
        gm[rows, :] = jnp.zeros((BLOCK, width), bf16)
        att[rows, :] = jnp.zeros((BLOCK, inner), bf16)
        return carry

    lax.fori_loop(0, nblk, clear, 0)

    def gather(i, carry):
        patch_copy(i).wait()
        cot_copy(i).wait()
        off = pl.multiple_of(offs[i], 16)
        kept_row = kept[pl.ds(i, 1), :]
        patch_ids = lax.broadcasted_iota(jnp.int32, (pbuf.shape[1], KEYS), 0)
        onehot = jnp.where(patch_ids == kept_row, 1.0, 0.0).astype(bf16)
        vis[pl.ds(off, KEYS), :] = dot(onehot, pbuf[i], TN).astype(bf16)
        live = lax.broadcasted_iota(jnp.int32, (ROWS, width), 0) < counts[i]
        gm[pl.ds(off, ROWS), :] = jnp.where(live, cbuf[i], jnp.zeros((ROWS, width), bf16))
        return carry

    lax.fori_loop(0, images, gather, 0)

    def out_copies(b, which=(0, 1, 2, 3, 4)):
        rows = row_block(b)
        pairs_of = ((vis, vis_o), (gm, gm_o), (qkv, qkv_o), (att, att_o), (mid, mid_o))
        return [
            pltpu.make_async_copy(pairs_of[n][0].at[rows], pairs_of[n][1].at[rows], blk_sem.at[n, b])
            for n in which
        ]

    def project(b, carry):
        rows = row_block(b)
        normed, _ = norm_stats(vis[rows, :].astype(f32))
        source = (normed * vec[0:1, :] + vec[2:3, :]).astype(bf16)
        for j in range(3):
            cols = slice(j * inner, (j + 1) * inner)
            part = dot(source, wqkv[:, cols])
            if j == 0:
                part = (part + bias[0:1, :]) * (HD**-0.5)
            if j == 2:
                part = part + bias[1:2, :]
            qkv[rows, cols] = part.astype(bf16)
        for copy in out_copies(b, (0, 1, 2)):
            copy.start()
        return carry

    lax.fori_loop(0, nblk, project, 0)

    def prob_copy(i):
        return pltpu.make_async_copy(prob.at[i], prob_o.at[i], prob_sem.at[i])

    def attend(i, carry):
        off = pl.multiple_of(offs[i], 16)
        count = counts[i]
        key_live = lax.broadcasted_iota(jnp.int32, (ROWS, KEYS), 1) < count
        row_live = lax.broadcasted_iota(jnp.int32, (ROWS, 1), 0) < count
        for p in range(pairs):
            c = p * KEYS
            q2 = qkv[pl.ds(off, ROWS), c : c + KEYS]
            k2 = qkv[pl.ds(off, KEYS), inner + c : inner + c + KEYS]
            v2 = qkv[pl.ds(off, KEYS), 2 * inner + c : 2 * inner + c + KEYS]
            scores = dot(q2, lane_split(k2), NT)
            halves = []
            for h in range(2):
                s = jnp.where(key_live, scores[:, h * KEYS : (h + 1) * KEYS], -1e30)
                e = jnp.exp(s - jnp.max(s, axis=-1, keepdims=True))
                r = jnp.where(row_live, 1.0 / jnp.sum(e, axis=-1, keepdims=True), 0.0)
                halves.append((e * r).astype(bf16))
            pr = jnp.concatenate(halves, axis=1)
            prob[i, :, 2 * c : 2 * c + 2 * KEYS] = pr
            att[pl.ds(off, ROWS), c : c + KEYS] = dot(pr, lane_split(v2)).astype(bf16)
        prob_copy(i).start()
        return carry

    lax.fori_loop(0, images, attend, 0)

    def finish(b, carry):
        rows = row_block(b)
        attention = dot(att[rows, :], wproj[...], NT) + vec[3:4, :]
        mid[rows, :] = vis[rows, :].astype(f32) + attention
        for copy in out_copies(b, (3, 4)):
            copy.start()
        return carry

    lax.fori_loop(0, nblk, finish, 0)

    def drain(b, carry):
        for copy in out_copies(b):
            copy.wait()
        return carry

    lax.fori_loop(0, nblk, drain, 0)

    def drain_prob(i, carry):
        prob_copy(i).wait()
        return carry

    lax.fori_loop(0, images, drain_prob, 0)


def mlp_kernel(
    images, groups, me_ref, counts, mid_h, gm_h, fc1, fc2, vec, bias,
    out_o, gmid_o, g1_o, g2_o, gb_o, small_o,
    offs, mid, gm, out, stage, in_sem, gmid_sem, out_sem,
):
    width = mid.shape[1]
    unit = fc1.shape[2]
    me = me_ref[0]
    fill_offsets(counts, offs, images)
    nblk = block_count(offs, images)

    def in_copies(b):
        rows = row_block(b)
        return (
            pltpu.make_async_copy(mid_h.at[rows], mid.at[rows], in_sem.at[0, b]),
            pltpu.make_async_copy(gm_h.at[rows], gm.at[rows], in_sem.at[1, b]),
        )

    def start_in(b, carry):
        for copy in in_copies(b):
            copy.start()
        return carry

    lax.fori_loop(0, nblk, start_in, 0)
    g1_o[...] = jnp.zeros_like(g1_o)
    g2_o[...] = jnp.zeros_like(g2_o)
    gb_o[...] = jnp.zeros_like(gb_o)
    small_o[...] = jnp.zeros_like(small_o)

    def gmid_copy(b):
        rows = row_block(b)
        return pltpu.make_async_copy(mid.at[rows], gmid_o.at[rows], gmid_sem.at[b])

    def block(b, carry):
        rows = row_block(b)
        for copy in in_copies(b):
            copy.wait()
        normed, inverse = norm_stats(mid[rows, :])
        source = (normed * vec[1:2, :] + vec[4:5, :]).astype(bf16)
        gmb = gm[rows, :]
        mlp = jnp.zeros((BLOCK, width), f32)
        gnm = jnp.zeros((BLOCK, width), f32)
        for s in range(groups):
            g = lax.rem(me + s, groups)
            w1 = fc1[g]
            w2 = fc2[g]
            pre = dot(source, w1) + bias[pl.ds(g, 1), :]
            act, slope = gelu_parts(pre)
            act = act.astype(bf16)
            gp = (dot(gmb, w2) * slope).astype(bf16)
            mlp = mlp + dot(act, w2, NT)
            gnm = gnm + dot(gp, w1, NT)
            if s == 0:
                g1_o[...] += dot(source, gp, TN)
                g2_o[...] += dot(gmb, act, TN)
                gb_o[...] += fold_rows(gp.astype(f32))
        out[rows, :] = (mid[rows, :] + mlp + vec[5:6, :]).astype(bf16)
        grad_mid = gmb.astype(f32) + norm_pull(gnm, normed, inverse, vec[1:2, :])
        small_o[0] += fold_rows(gnm * normed)
        small_o[1] += fold_rows(gnm)
        small_o[2] += fold_rows(gmb.astype(f32))
        mid[rows, :] = grad_mid
        gmid_copy(b).start()
        return carry

    lax.fori_loop(0, nblk, block, 0)

    def out_copy(i):
        return pltpu.make_async_copy(stage.at[i], out_o.at[i], out_sem.at[i])

    def unpack(i, carry):
        off = pl.multiple_of(offs[i], 16)
        slots = stage.shape[1]
        live = lax.broadcasted_iota(jnp.int32, (ROWS, width), 0) < counts[i]
        stage[i, pl.ds(0, ROWS), :] = jnp.where(live, out[pl.ds(off, ROWS), :], jnp.zeros((ROWS, width), bf16))
        if slots > ROWS:
            stage[i, pl.ds(ROWS, slots - ROWS), :] = jnp.zeros((slots - ROWS, width), bf16)
        out_copy(i).start()
        return carry

    lax.fori_loop(0, images, unpack, 0)

    def drain(i, carry):
        out_copy(i).wait()
        return carry

    lax.fori_loop(0, images, drain, 0)

    def drain_gmid(b, carry):
        gmid_copy(b).wait()
        return carry

    lax.fori_loop(0, nblk, drain_gmid, 0)


def back_kernel(
    images, pairs, me_ref, counts, kept, gmid_h, qkv_h, att_h, prob_h, vis_h, wqkv, wproj, vec,
    pg_o, gq_o, gp_o, small_o, qb_o,
    offs, gmid, qkv, att, prob, vis, gat, dqkv, accq, accp, stage,
    in_sem, prob_sem, pg_sem,
):
    width = vis.shape[1]
    inner = gat.shape[1]
    me = me_ref[0]
    own = gp_o.shape[1]
    window = accp.shape[1]
    start = pl.multiple_of(lax.div(me * own, KEYS) * KEYS, KEYS)
    fill_offsets(counts, offs, images)
    nblk = block_count(offs, images)

    def in_copies(b, which=(0, 1, 2, 3)):
        rows = row_block(b)
        pairs_of = (
            (gmid_h.at[rows], gmid),
            (att_h.at[rows, pl.ds(start, window)], att),
            (qkv_h.at[rows], qkv),
            (vis_h.at[rows], vis),
        )
        return [
            pltpu.make_async_copy(pairs_of[n][0], pairs_of[n][1].at[rows], in_sem.at[n, b])
            for n in which
        ]

    def start_in(b, carry):
        for copy in in_copies(b):
            copy.start()
        return carry

    lax.fori_loop(0, nblk, start_in, 0)
    accq[...] = jnp.zeros_like(accq)
    accp[...] = jnp.zeros_like(accp)
    small_o[...] = jnp.zeros_like(small_o)
    qb_o[...] = jnp.zeros_like(qb_o)

    def first(b, carry):
        rows = row_block(b)
        for copy in in_copies(b, (0, 1)):
            copy.wait()
        ga = gmid[rows, :].astype(bf16)
        small_o[1] += fold_rows(ga.astype(f32))
        gat[rows, :] = dot(ga, wproj[...]).astype(bf16)
        accp[...] += dot(ga, att[rows, :], TN)
        dqkv[rows, :] = jnp.zeros((BLOCK, dqkv.shape[1]), bf16)
        return carry

    lax.fori_loop(0, nblk, first, 0)

    def wait_rest(b, carry):
        for copy in in_copies(b, (2, 3)):
            copy.wait()
        return carry

    lax.fori_loop(0, nblk, wait_rest, 0)

    def prob_copy(i):
        slot = lax.rem(i, 2)
        return pltpu.make_async_copy(prob_h.at[i], prob.at[slot], prob_sem.at[slot])

    prob_copy(0).start()

    def attend(i, carry):
        off = pl.multiple_of(offs[i], 16)
        slot = lax.rem(i, 2)
        prob_copy(i).wait()

        @pl.when(i + 1 < images)
        def _():
            prob_copy(i + 1).start()

        left = lax.broadcasted_iota(jnp.int32, (ROWS, KEYS), 1) < HD
        for p in range(pairs):
            c = p * KEYS
            q2 = qkv[pl.ds(off, ROWS), c : c + KEYS]
            k2 = qkv[pl.ds(off, KEYS), inner + c : inner + c + KEYS]
            v2 = qkv[pl.ds(off, KEYS), 2 * inner + c : 2 * inner + c + KEYS]
            do2 = gat[pl.ds(off, ROWS), c : c + KEYS]
            pr = prob[slot, :, 2 * c : 2 * c + 2 * KEYS]
            dp = dot(do2, lane_split(v2), NT)
            halves = []
            for h in range(2):
                ph = pr[:, h * KEYS : (h + 1) * KEYS].astype(f32)
                dh = dp[:, h * KEYS : (h + 1) * KEYS]
                delta = jnp.sum(ph * dh, axis=-1, keepdims=True)
                halves.append((ph * (dh - delta)).astype(bf16))
            gs = jnp.concatenate(halves, axis=1)
            dq = dot(gs, lane_split(k2)) * (HD**-0.5)
            dk = dot(gs, q2, TN)
            dv = dot(pr, do2, TN)
            dqkv[pl.ds(off, ROWS), c : c + KEYS] = dq.astype(bf16)
            dqkv[pl.ds(off, ROWS), inner + c : inner + c + KEYS] = jnp.where(
                left, dk[:ROWS], dk[KEYS : KEYS + ROWS]
            ).astype(bf16)
            dqkv[pl.ds(off, ROWS), 2 * inner + c : 2 * inner + c + KEYS] = jnp.where(
                left, dv[:ROWS], dv[KEYS : KEYS + ROWS]
            ).astype(bf16)
        return carry

    lax.fori_loop(0, images, attend, 0)

    def second(b, carry):
        rows = row_block(b)
        normed, inverse = norm_stats(vis[rows, :].astype(f32))
        source = (normed * vec[0:1, :] + vec[2:3, :]).astype(bf16)
        gni = dot(dqkv[rows, :], wqkv[...], NT)
        small_o[0] += fold_rows(gni * normed)
        small_o[2] += fold_rows(gni)
        for j in range(3):
            mine = dqkv[rows, pl.ds(pl.multiple_of(j * inner + start, KEYS), window)]
            accq[j] += dot(source, mine, TN)
            if j == 0:
                qb_o[0] += fold_rows(mine.astype(f32))
            if j == 2:
                qb_o[1] += fold_rows(mine.astype(f32))
        grad = gmid[rows, :] + norm_pull(gni, normed, inverse, vec[0:1, :])
        gat[rows, :] = grad.astype(bf16)
        return carry

    lax.fori_loop(0, nblk, second, 0)

    slots = stage.shape[0]

    def pg_copy(i):
        slot = lax.rem(i, slots)
        return pltpu.make_async_copy(stage.at[slot], pg_o.at[i], pg_sem.at[slot])

    def scatter(i, carry):
        @pl.when(i >= slots)
        def _():
            pg_copy(i - slots).wait()

        off = pl.multiple_of(offs[i], 16)
        kept_row = kept[pl.ds(i, 1), :]
        shape = (stage.shape[1], KEYS)
        hit = (lax.broadcasted_iota(jnp.int32, shape, 0) == kept_row) & (
            lax.broadcasted_iota(jnp.int32, shape, 1) < counts[i]
        )
        onehot = jnp.where(hit, 1.0, 0.0).astype(bf16)
        stage[lax.rem(i, slots)] = dot(onehot, gat[pl.ds(off, KEYS), :])
        pg_copy(i).start()
        return carry

    lax.fori_loop(0, images, scatter, 0)

    def drain(i, carry):
        pg_copy(i).wait()
        return carry

    lax.fori_loop(max(0, images - slots), images, drain, 0)

    def emit(shift):
        gp_o[...] = accp[:, shift : shift + own]
        for j in range(3):
            gq_o[j] = accq[j, :, shift : shift + own]

    shift = me * own - start

    @pl.when(shift == 0)
    def _():
        emit(0)

    @pl.when(shift != 0)
    def _():
        emit(window - own)


SMEM = pl.BlockSpec(memory_space=pltpu.SMEM)
VMEM = pl.BlockSpec(memory_space=pltpu.VMEM)
ANY = pl.BlockSpec(memory_space=pl.ANY)
PARAMS = dict(compiler_params=pltpu.CompilerParams(vmem_limit_bytes=VMEM_BYTES))


def struct(shape, dtype):
    return jax.ShapeDtypeStruct(shape, dtype)


def run_group(patches, counts, kept, cot, vec, qkv_b, fc1_b, wqkv, wproj, fc1, fc2, me, own):
    images, patch_count, width = patches.shape
    slot_count = cot.shape[1]
    inner = wproj.shape[1]
    pairs = inner // KEYS
    groups, _, unit = fc1.shape
    cap = -(-((images - 1) * ROWS + KEYS) // BLOCK) * BLOCK
    nmax = cap // BLOCK
    dma = pltpu.SemaphoreType.DMA
    vis, gm, qkv, att, prob, mid = pl.pallas_call(
        functools.partial(attend_kernel, images, pairs),
        name="attend",
        in_specs=[SMEM, VMEM, ANY, ANY, VMEM, VMEM, VMEM, VMEM],
        out_specs=[ANY] * 6,
        out_shape=[
            struct((cap, width), bf16),
            struct((cap, width), bf16),
            struct((cap, 3 * inner), bf16),
            struct((cap, inner), bf16),
            struct((images, ROWS, 2 * pairs * KEYS), bf16),
            struct((cap, width), f32),
        ],
        scratch_shapes=[
            pltpu.SMEM((images,), jnp.int32),
            pltpu.VMEM((images, patch_count, width), bf16),
            pltpu.VMEM((images, ROWS, width), bf16),
            pltpu.VMEM((cap, width), bf16),
            pltpu.VMEM((cap, width), bf16),
            pltpu.VMEM((cap, 3 * inner), bf16),
            pltpu.VMEM((cap, inner), bf16),
            pltpu.VMEM((images, ROWS, 2 * pairs * KEYS), bf16),
            pltpu.VMEM((cap, width), f32),
            dma((images,)),
            dma((images,)),
            dma((5, nmax)),
            dma((images,)),
        ],
        **PARAMS,
    )(counts, kept, patches, cot, wqkv, wproj, vec, qkv_b)
    out, gmid, g1, g2, gb, small2 = pl.pallas_call(
        functools.partial(mlp_kernel, images, groups),
        name="mlp",
        in_specs=[SMEM, SMEM, ANY, ANY, VMEM, VMEM, VMEM, VMEM],
        out_specs=[ANY, ANY, VMEM, VMEM, VMEM, VMEM],
        out_shape=[
            struct((images, slot_count, width), bf16),
            struct((cap, width), f32),
            struct((width, unit), f32),
            struct((width, unit), f32),
            struct((8, unit), f32),
            struct((3, 8, width), f32),
        ],
        scratch_shapes=[
            pltpu.SMEM((images,), jnp.int32),
            pltpu.VMEM((cap, width), f32),
            pltpu.VMEM((cap, width), bf16),
            pltpu.VMEM((cap, width), bf16),
            pltpu.VMEM((images, slot_count, width), bf16),
            dma((2, nmax)),
            dma((nmax,)),
            dma((images,)),
        ],
        **PARAMS,
    )(me, counts, mid, gm, fc1, fc2, vec, fc1_b)
    window = -(-own // KEYS) * KEYS
    pg, gq, gp, small3, qb = pl.pallas_call(
        functools.partial(back_kernel, images, pairs),
        name="back",
        in_specs=[SMEM, SMEM, VMEM, ANY, ANY, ANY, ANY, ANY, VMEM, VMEM, VMEM],
        out_specs=[ANY, VMEM, VMEM, VMEM, VMEM],
        out_shape=[
            struct((images, patch_count, width), f32),
            struct((3, width, own), f32),
            struct((width, own), f32),
            struct((3, 8, width), f32),
            struct((2, 8, window), f32),
        ],
        scratch_shapes=[
            pltpu.SMEM((images,), jnp.int32),
            pltpu.VMEM((cap, width), f32),
            pltpu.VMEM((cap, 3 * inner), bf16),
            pltpu.VMEM((cap, window), bf16),
            pltpu.VMEM((2, ROWS, 2 * pairs * KEYS), bf16),
            pltpu.VMEM((cap, width), bf16),
            pltpu.VMEM((cap, inner), bf16),
            pltpu.VMEM((cap, 3 * inner), bf16),
            pltpu.VMEM((3, width, window), f32),
            pltpu.VMEM((width, window), f32),
            pltpu.VMEM((2, patch_count, width), f32),
            dma((4, nmax)),
            dma((2,)),
            dma((2,)),
        ],
        **PARAMS,
    )(me, counts, kept, gmid, qkv, att, prob, vis, wqkv, wproj, vec)
    shift = jnp.where(me[0] * own % KEYS == 0, 0, window - own)
    qb = lax.dynamic_slice_in_dim(jnp.sum(qb, axis=1), shift, own, 1)
    small2 = jnp.sum(small2, axis=1)
    small3 = jnp.sum(small3, axis=1)
    small = jnp.stack([small3[0], small2[0], small3[2], small3[1], small2[1], small2[2]])
    return out, pg, (small, gq, gp, g1, g2, qb, jnp.sum(gb, axis=0))


def per_device(
    patches,
    counts,
    kept_patches,
    cotangent,
    norm_gains,
    shifts,
    qkv_weight,
    qkv_bias,
    proj_weight,
    fc1_weight,
    fc1_bias,
    fc2_weight,
):
    image_count, patch_count, width = patches.shape
    n_mp = lax.axis_size("mp")
    me = lax.axis_index("mp").astype(jnp.int32).reshape(1)
    own = qkv_weight.shape[2]
    inner = own * n_mp

    vec = lax.all_gather(jnp.concatenate([norm_gains, shifts]), "dp", axis=1, tiled=True).astype(f32)
    vec = jnp.pad(vec, ((0, 2), (0, 0)))
    qkv = lax.all_gather(lax.all_gather(qkv_weight, "mp", axis=2, tiled=True), "dp", axis=0, tiled=True)
    qkv = qkv.reshape(width, 3 * inner)
    qkv_b = lax.all_gather(qkv_bias, "mp", axis=1, tiled=True).astype(f32)
    proj = lax.all_gather(lax.all_gather(proj_weight.T, "mp", axis=1, tiled=True), "dp", axis=0, tiled=True)
    fc1 = lax.all_gather(lax.all_gather(fc1_weight, "mp", axis=0), "dp", axis=1, tiled=True)
    fc1_b = lax.all_gather(fc1_bias, "mp", axis=0).astype(f32)
    fc2 = lax.all_gather(lax.all_gather(fc2_weight.T, "mp", axis=0), "dp", axis=1, tiled=True)

    group = max(n for n in range(1, GROUP_MAX + 1) if image_count % n == 0)
    outs, pgs, totals = [], [], None
    for first in range(0, image_count, group):
        part = slice(first, first + group)
        out, pg, grads = run_group(
            patches[part], counts[part], kept_patches[part], cotangent[part],
            vec, qkv_b, fc1_b, qkv, proj, fc1, fc2, me, own,
        )
        outs.append(out)
        pgs.append(pg)
        totals = grads if totals is None else tuple(a + b for a, b in zip(totals, grads))
    small, g_qkv, g_proj, g_fc1, g_fc2, g_qb, g_fc1b = totals
    hid = g_fc1.shape[1]
    big = jnp.concatenate([g_qkv[0], g_qkv[1], g_qkv[2], g_proj, g_fc1, g_fc2], axis=1).astype(bf16)
    big = lax.psum_scatter(big, "dp", scatter_dimension=0, tiled=True).astype(f32)
    a, b, c = 3 * own, 4 * own, 4 * own + hid
    small = lax.psum_scatter(small, "dp", scatter_dimension=1, tiled=True)
    g_qb, g_fc1b = lax.psum((g_qb, g_fc1b), "dp")
    return (
        outs[0] if len(outs) == 1 else jnp.concatenate(outs, axis=0),
        pgs[0] if len(pgs) == 1 else jnp.concatenate(pgs, axis=0),
        small[:2],
        small[2:],
        big[:, :a].reshape(-1, 3, own),
        g_qb,
        big[:, a:b].T,
        big[:, b:c],
        g_fc1b,
        big[:, c:].T,
    )


def solution(mesh):
    placed = (
        P("dp", None, None),
        P("dp"),
        P("dp", None),
        P("dp", None, None),
        P(None, "dp"),
        P(None, "dp"),
        P("dp", None, "mp"),
        P(None, "mp"),
        P("mp", "dp"),
        P("dp", "mp"),
        P("mp"),
        P("mp", "dp"),
    )
    return jax.shard_map(
        per_device,
        mesh=mesh,
        in_specs=placed,
        out_specs=(
            P("dp", None, None),
            P("dp", None, None),
            P(None, "dp"),
            P(None, "dp"),
            P("dp", None, "mp"),
            P(None, "mp"),
            P("mp", "dp"),
            P("dp", "mp"),
            P("mp"),
            P("mp", "dp"),
        ),
        check_vma=False,
    )
```

```python
import functools

import jax
import jax.numpy as jnp
from jax import lax
from jax.experimental import pallas as pl
from jax.experimental.pallas import tpu as pltpu
from jax.sharding import PartitionSpec as P

HD = 64
KEEP_MAX = 98
ROWS = 112
KEYS = 128
BLOCK = 256
GROUP_MAX = 24
EPSILON = 1e-06
VMEM_BYTES = 59 * 2**20

f32 = jnp.float32
bf16 = jnp.bfloat16

NN = (((1,), (0,)), ((), ()))
NT = (((1,), (1,)), ((), ()))
TN = (((0,), (0,)), ((), ()))


def dot(left, right, dims=NN):
    return lax.dot_general(left, right, dims, preferred_element_type=f32)


def norm_stats(values):
    row_mean = jnp.mean(values, axis=-1, keepdims=True)
    centred = values - row_mean
    inverse = lax.rsqrt(jnp.mean(centred * centred, axis=-1, keepdims=True) + EPSILON)
    return centred * inverse, inverse


def norm_pull(grad_normed, normed, inverse, gain_row):
    scaled = grad_normed * gain_row
    first_mean = jnp.mean(scaled, axis=-1, keepdims=True)
    second_mean = jnp.mean(scaled * normed, axis=-1, keepdims=True)
    return inverse * (scaled - first_mean - normed * second_mean)


def fold_rows(values):
    rows, width = values.shape
    return jnp.sum(values.reshape(rows // 8, 8, width), axis=0)


def gelu_parts(u):
    bell = jnp.exp(u * u * -0.5)
    t = 1.0 / (1.0 + 0.23164190 * jnp.abs(u))
    poly = 0.5307027145
    for c in (-0.7265760135, 0.7107068705, -0.142248368, 0.127414796):
        poly = poly * t + c
    tail = poly * t * bell
    cdf = jnp.where(u >= 0, 1.0 - tail, tail)
    return u * cdf, cdf + u * bell * 0.3989422804014327


def fill_offsets(counts, offs, images):
    def step(i, total):
        offs[i] = total
        return total + lax.div(counts[i] + 15, 16) * 16

    return lax.fori_loop(0, images, step, 0)


def block_count(offs, images):
    return lax.div(offs[images - 1] + KEYS + BLOCK - 1, BLOCK)


def lane_split(values):
    left = lax.broadcasted_iota(jnp.int32, values.shape, 1) < HD
    zero = jnp.zeros_like(values)
    return jnp.concatenate([jnp.where(left, values, zero), jnp.where(left, zero, values)], axis=0)


def row_block(b):
    return pl.ds(pl.multiple_of(b * BLOCK, BLOCK), BLOCK)


def attend_kernel(
    images, pairs, counts, kept, patches, cot, wqkv, wproj, vec, bias,
    vis_o, gm_o, qkv_o, att_o, prob_o, mid_o,
    offs, pbuf, cbuf, vis, gm, qkv, att, prob, mid, in_sem, cot_sem, blk_sem, prob_sem,
):
    width = vis.shape[1]
    inner = att.shape[1]
    fill_offsets(counts, offs, images)
    nblk = block_count(offs, images)

    def patch_copy(i):
        return pltpu.make_async_copy(patches.at[i], pbuf.at[i], in_sem.at[i])

    def cot_copy(i):
        return pltpu.make_async_copy(cot.at[i, pl.ds(0, ROWS)], cbuf.at[i], cot_sem.at[i])

    def start_in(i, carry):
        patch_copy(i).start()
        cot_copy(i).start()
        return carry

    lax.fori_loop(0, images, start_in, 0)

    def clear(b, carry):
        rows = row_block(b)
        vis[rows, :] = jnp.zeros((BLOCK, width), bf16)
        gm[rows, :] = jnp.zeros((BLOCK, width), bf16)
        att[rows, :] = jnp.zeros((BLOCK, inner), bf16)
        return carry

    lax.fori_loop(0, nblk, clear, 0)

    def gather(i, carry):
        patch_copy(i).wait()
        cot_copy(i).wait()
        off = pl.multiple_of(offs[i], 16)
        kept_row = kept[pl.ds(i, 1), :]
        patch_ids = lax.broadcasted_iota(jnp.int32, (pbuf.shape[1], KEYS), 0)
        onehot = jnp.where(patch_ids == kept_row, 1.0, 0.0).astype(bf16)
        vis[pl.ds(off, KEYS), :] = dot(onehot, pbuf[i], TN).astype(bf16)
        live = lax.broadcasted_iota(jnp.int32, (ROWS, width), 0) < counts[i]
        gm[pl.ds(off, ROWS), :] = jnp.where(live, cbuf[i], jnp.zeros((ROWS, width), bf16))
        return carry

    lax.fori_loop(0, images, gather, 0)

    def out_copies(b, which=(0, 1, 2, 3, 4)):
        rows = row_block(b)
        pairs_of = ((vis, vis_o), (gm, gm_o), (qkv, qkv_o), (att, att_o), (mid, mid_o))
        return [
            pltpu.make_async_copy(pairs_of[n][0].at[rows], pairs_of[n][1].at[rows], blk_sem.at[n, b])
            for n in which
        ]

    def project(b, carry):
        rows = row_block(b)
        normed, _ = norm_stats(vis[rows, :].astype(f32))
        source = (normed * vec[0:1, :] + vec[2:3, :]).astype(bf16)
        for j in range(3):
            cols = slice(j * inner, (j + 1) * inner)
            part = dot(source, wqkv[:, cols])
            if j == 0:
                part = (part + bias[0:1, :]) * (HD**-0.5)
            if j == 2:
                part = part + bias[1:2, :]
            qkv[rows, cols] = part.astype(bf16)
        for copy in out_copies(b, (0, 1, 2)):
            copy.start()
        return carry

    lax.fori_loop(0, nblk, project, 0)

    def prob_copy(i):
        return pltpu.make_async_copy(prob.at[i], prob_o.at[i], prob_sem.at[i])

    def attend(i, carry):
        off = pl.multiple_of(offs[i], 16)
        count = counts[i]
        key_live = lax.broadcasted_iota(jnp.int32, (ROWS, KEYS), 1) < count
        row_live = lax.broadcasted_iota(jnp.int32, (ROWS, 1), 0) < count
        for p in range(pairs):
            c = p * KEYS
            q2 = qkv[pl.ds(off, ROWS), c : c + KEYS]
            k2 = qkv[pl.ds(off, KEYS), inner + c : inner + c + KEYS]
            v2 = qkv[pl.ds(off, KEYS), 2 * inner + c : 2 * inner + c + KEYS]
            scores = dot(q2, lane_split(k2), NT)
            halves = []
            for h in range(2):
                s = jnp.where(key_live, scores[:, h * KEYS : (h + 1) * KEYS], -1e30)
                e = jnp.exp(s - jnp.max(s, axis=-1, keepdims=True))
                r = jnp.where(row_live, 1.0 / jnp.sum(e, axis=-1, keepdims=True), 0.0)
                halves.append((e * r).astype(bf16))
            pr = jnp.concatenate(halves, axis=1)
            prob[i, :, 2 * c : 2 * c + 2 * KEYS] = pr
            att[pl.ds(off, ROWS), c : c + KEYS] = dot(pr, lane_split(v2)).astype(bf16)
        prob_copy(i).start()
        return carry

    lax.fori_loop(0, images, attend, 0)

    def finish(b, carry):
        rows = row_block(b)
        attention = dot(att[rows, :], wproj[...], NT) + vec[3:4, :]
        mid[rows, :] = vis[rows, :].astype(f32) + attention
        for copy in out_copies(b, (3, 4)):
            copy.start()
        return carry

    lax.fori_loop(0, nblk, finish, 0)

    def drain(b, carry):
        for copy in out_copies(b):
            copy.wait()
        return carry

    lax.fori_loop(0, nblk, drain, 0)

    def drain_prob(i, carry):
        prob_copy(i).wait()
        return carry

    lax.fori_loop(0, images, drain_prob, 0)


def mlp_kernel(
    images, groups, me_ref, counts, mid_h, gm_h, fcs, vec, bias,
    out_o, gmid_o, gfc_o, gb_o, small_o,
    offs, mid, gm, out, stage, acc, in_sem, gmid_sem, out_sem,
):
    width = mid.shape[1]
    me = me_ref[0]
    fill_offsets(counts, offs, images)
    nblk = block_count(offs, images)

    def in_copies(b):
        rows = row_block(b)
        return (
            pltpu.make_async_copy(mid_h.at[rows], mid.at[rows], in_sem.at[0, b]),
            pltpu.make_async_copy(gm_h.at[rows], gm.at[rows], in_sem.at[1, b]),
        )

    def start_in(b, carry):
        for copy in in_copies(b):
            copy.start()
        return carry

    lax.fori_loop(0, nblk, start_in, 0)
    acc[...] = jnp.zeros_like(acc)
    gb_o[...] = jnp.zeros_like(gb_o)
    small_o[...] = jnp.zeros_like(small_o)

    def gmid_copy(b):
        rows = row_block(b)
        return pltpu.make_async_copy(mid.at[rows], gmid_o.at[rows], gmid_sem.at[b])

    def block(b, carry):
        rows = row_block(b)
        for copy in in_copies(b):
            copy.wait()
        normed, inverse = norm_stats(mid[rows, :])
        source = (normed * vec[1:2, :] + vec[4:5, :]).astype(bf16)
        gmb = gm[rows, :]
        mlp = jnp.zeros((BLOCK, width), f32)
        gnm = jnp.zeros((BLOCK, width), f32)
        for s in range(groups):
            g = lax.rem(me + s, groups)
            w1 = fcs[0, g]
            w2 = fcs[1, g]
            pre = dot(source, w1) + bias[pl.ds(g, 1), :]
            act, slope = gelu_parts(pre)
            act = act.astype(bf16)
            gp = (dot(gmb, w2) * slope).astype(bf16)
            mlp = mlp + dot(act, w2, NT)
            gnm = gnm + dot(gp, w1, NT)
            if s == 0:
                acc[0] += dot(source, gp, TN)
                acc[1] += dot(gmb, act, TN)
                gb_o[...] += fold_rows(gp.astype(f32))
        out[rows, :] = (mid[rows, :] + mlp + vec[5:6, :]).astype(bf16)
        grad_mid = gmb.astype(f32) + norm_pull(gnm, normed, inverse, vec[1:2, :])
        small_o[0] += fold_rows(gnm * normed)
        small_o[1] += fold_rows(gnm)
        small_o[2] += fold_rows(gmb.astype(f32))
        mid[rows, :] = grad_mid
        gmid_copy(b).start()
        return carry

    lax.fori_loop(0, nblk, block, 0)
    for n in range(2):
        gfc_o[:, n * acc.shape[2] : (n + 1) * acc.shape[2]] = acc[n].astype(bf16)

    def out_copy(i):
        return pltpu.make_async_copy(stage.at[i], out_o.at[i], out_sem.at[i])

    def unpack(i, carry):
        off = pl.multiple_of(offs[i], 16)
        slots = stage.shape[1]
        live = lax.broadcasted_iota(jnp.int32, (ROWS, width), 0) < counts[i]
        stage[i, pl.ds(0, ROWS), :] = jnp.where(live, out[pl.ds(off, ROWS), :], jnp.zeros((ROWS, width), bf16))
        if slots > ROWS:
            stage[i, pl.ds(ROWS, slots - ROWS), :] = jnp.zeros((slots - ROWS, width), bf16)
        out_copy(i).start()
        return carry

    lax.fori_loop(0, images, unpack, 0)

    def drain(i, carry):
        out_copy(i).wait()
        return carry

    lax.fori_loop(0, images, drain, 0)

    def drain_gmid(b, carry):
        gmid_copy(b).wait()
        return carry

    lax.fori_loop(0, nblk, drain_gmid, 0)


def back_kernel(
    images, pairs, me_ref, counts, kept, gmid_h, qkv_h, att_h, prob_h, vis_h, wqkv, wproj, vec,
    pg_o, ga_o, small_o, qb_o,
    offs, gmid, qkv, att, prob, vis, gat, dqkv, accq, accp, qsum, stage,
    in_sem, prob_sem, pg_sem,
):
    width = vis.shape[1]
    inner = gat.shape[1]
    me = me_ref[0]
    own = qb_o.shape[2]
    window = accp.shape[1]
    start = pl.multiple_of(lax.div(me * own, KEYS) * KEYS, KEYS)
    fill_offsets(counts, offs, images)
    nblk = block_count(offs, images)

    def in_copies(b, which=(0, 1, 2, 3)):
        rows = row_block(b)
        pairs_of = (
            (gmid_h.at[rows], gmid),
            (att_h.at[rows, pl.ds(start, window)], att),
            (qkv_h.at[rows], qkv),
            (vis_h.at[rows], vis),
        )
        return [
            pltpu.make_async_copy(pairs_of[n][0], pairs_of[n][1].at[rows], in_sem.at[n, b])
            for n in which
        ]

    def start_in(b, carry):
        for copy in in_copies(b):
            copy.start()
        return carry

    lax.fori_loop(0, nblk, start_in, 0)
    accq[...] = jnp.zeros_like(accq)
    accp[...] = jnp.zeros_like(accp)
    small_o[...] = jnp.zeros_like(small_o)
    qsum[...] = jnp.zeros_like(qsum)

    def first(b, carry):
        rows = row_block(b)
        for copy in in_copies(b, (0, 1)):
            copy.wait()
        ga = gmid[rows, :].astype(bf16)
        small_o[1] += fold_rows(ga.astype(f32))
        gat[rows, :] = dot(ga, wproj[...]).astype(bf16)
        accp[...] += dot(ga, att[rows, :], TN)
        dqkv[rows, :] = jnp.zeros((BLOCK, dqkv.shape[1]), bf16)
        return carry

    lax.fori_loop(0, nblk, first, 0)

    def wait_rest(b, carry):
        for copy in in_copies(b, (2, 3)):
            copy.wait()
        return carry

    lax.fori_loop(0, nblk, wait_rest, 0)

    def prob_copy(i):
        slot = lax.rem(i, 2)
        return pltpu.make_async_copy(prob_h.at[i], prob.at[slot], prob_sem.at[slot])

    prob_copy(0).start()

    def attend(i, carry):
        off = pl.multiple_of(offs[i], 16)
        slot = lax.rem(i, 2)
        prob_copy(i).wait()

        @pl.when(i + 1 < images)
        def _():
            prob_copy(i + 1).start()

        left = lax.broadcasted_iota(jnp.int32, (ROWS, KEYS), 1) < HD
        for p in range(pairs):
            c = p * KEYS
            q2 = qkv[pl.ds(off, ROWS), c : c + KEYS]
            k2 = qkv[pl.ds(off, KEYS), inner + c : inner + c + KEYS]
            v2 = qkv[pl.ds(off, KEYS), 2 * inner + c : 2 * inner + c + KEYS]
            do2 = gat[pl.ds(off, ROWS), c : c + KEYS]
            pr = prob[slot, :, 2 * c : 2 * c + 2 * KEYS]
            dp = dot(do2, lane_split(v2), NT)
            halves = []
            for h in range(2):
                ph = pr[:, h * KEYS : (h + 1) * KEYS].astype(f32)
                dh = dp[:, h * KEYS : (h + 1) * KEYS]
                delta = jnp.sum(ph * dh, axis=-1, keepdims=True)
                halves.append((ph * (dh - delta)).astype(bf16))
            gs = jnp.concatenate(halves, axis=1)
            dq = dot(gs, lane_split(k2)) * (HD**-0.5)
            dk = dot(gs, q2, TN)
            dv = dot(pr, do2, TN)
            dqkv[pl.ds(off, ROWS), c : c + KEYS] = dq.astype(bf16)
            dqkv[pl.ds(off, ROWS), inner + c : inner + c + KEYS] = jnp.where(
                left, dk[:ROWS], dk[KEYS : KEYS + ROWS]
            ).astype(bf16)
            dqkv[pl.ds(off, ROWS), 2 * inner + c : 2 * inner + c + KEYS] = jnp.where(
                left, dv[:ROWS], dv[KEYS : KEYS + ROWS]
            ).astype(bf16)
        return carry

    lax.fori_loop(0, images, attend, 0)

    def second(b, carry):
        rows = row_block(b)
        normed, inverse = norm_stats(vis[rows, :].astype(f32))
        source = (normed * vec[0:1, :] + vec[2:3, :]).astype(bf16)
        gni = dot(dqkv[rows, :], wqkv[...], NT)
        small_o[0] += fold_rows(gni * normed)
        small_o[2] += fold_rows(gni)
        for j in range(3):
            mine = dqkv[rows, pl.ds(pl.multiple_of(j * inner + start, KEYS), window)]
            accq[j] += dot(source, mine, TN)
            if j == 0:
                qsum[0] += fold_rows(mine.astype(f32))
            if j == 2:
                qsum[1] += fold_rows(mine.astype(f32))
        grad = gmid[rows, :] + norm_pull(gni, normed, inverse, vec[0:1, :])
        gat[rows, :] = grad.astype(bf16)
        return carry

    lax.fori_loop(0, nblk, second, 0)

    slots = stage.shape[0]

    def pg_copy(i):
        slot = lax.rem(i, slots)
        return pltpu.make_async_copy(stage.at[slot], pg_o.at[i], pg_sem.at[slot])

    def scatter(i, carry):
        @pl.when(i >= slots)
        def _():
            pg_copy(i - slots).wait()

        off = pl.multiple_of(offs[i], 16)
        kept_row = kept[pl.ds(i, 1), :]
        shape = (stage.shape[1], KEYS)
        hit = (lax.broadcasted_iota(jnp.int32, shape, 0) == kept_row) & (
            lax.broadcasted_iota(jnp.int32, shape, 1) < counts[i]
        )
        onehot = jnp.where(hit, 1.0, 0.0).astype(bf16)
        stage[lax.rem(i, slots)] = dot(onehot, gat[pl.ds(off, KEYS), :])
        pg_copy(i).start()
        return carry

    lax.fori_loop(0, images, scatter, 0)

    def drain(i, carry):
        pg_copy(i).wait()
        return carry

    lax.fori_loop(max(0, images - slots), images, drain, 0)

    def emit(shift):
        ga_o[:, 3 * own : 4 * own] = accp[:, shift : shift + own].astype(bf16)
        for j in range(3):
            ga_o[:, j * own : (j + 1) * own] = accq[j, :, shift : shift + own].astype(bf16)
        for n in range(2):
            qb_o[n] = qsum[n, :, shift : shift + own]

    shift = me * own - start

    @pl.when(shift == 0)
    def _():
        emit(0)

    @pl.when(shift != 0)
    def _():
        emit(window - own)


SMEM = pl.BlockSpec(memory_space=pltpu.SMEM)
VMEM = pl.BlockSpec(memory_space=pltpu.VMEM)
ANY = pl.BlockSpec(memory_space=pl.ANY)
PARAMS = dict(compiler_params=pltpu.CompilerParams(vmem_limit_bytes=VMEM_BYTES))


def struct(shape, dtype):
    return jax.ShapeDtypeStruct(shape, dtype)


MESH = pl.DeviceIdType.MESH
SMALL_ROWS = 16


def greet(peers):
    barrier = pltpu.get_barrier_semaphore()
    for peer in peers:
        pl.semaphore_signal(barrier, inc=1, device_id=peer, device_id_type=MESH)
    pl.semaphore_wait(barrier, len(peers))


def gather_kernel(
    n_mp, qkv_w, proj_w, fc1_w, fc2_w, gains, shifts, qkv_b, fc1_b,
    wqkv_o, wproj_o, fcs, vec_o, qb_o, fb_o,
    held, wqkv, wproj, notes, own_sem, out_sem, send_sem, recv_sem,
):
    g = lax.axis_index("mp")
    d = lax.axis_index("dp")
    depth, width = fc1_w.shape
    part = qkv_w.shape[2]
    x_peer, y_peer, twin = d ^ 2, d ^ 4, d ^ 1
    across = [g ^ s for s in range(n_mp)]
    greet(
        [(d, across[s]) for s in range(1, n_mp)] + [(x_peer, g), (y_peer, g), (twin, g)]
    )
    own1 = pltpu.make_async_copy(fc1_w, fcs.at[0, g, d], own_sem.at[0])
    own2 = pltpu.make_async_copy(fc2_w, fcs.at[1, g, d], own_sem.at[1])
    own1.start()
    own2.start()
    for j in range(3):
        held[g, d, 0:depth, j * part : (j + 1) * part] = qkv_w[j]
    held[g, d, 0:depth, 3 * part : 4 * part] = proj_w[...].astype(f32).T.astype(bf16)
    notes[...] = jnp.zeros_like(notes)
    notes[0:2, 0:depth] = gains[...].astype(f32)
    notes[2:6, 0:depth] = shifts[...].astype(f32)
    notes[6:8, 0:part] = qkv_b[...].astype(f32)
    notes[8:9, :] = fc1_b[...].astype(f32)
    held[g, d, depth : depth + SMALL_ROWS, :] = notes[...].astype(bf16)

    half = width // 2
    halves = (slice(0, half), slice(half, width))
    firsts = (x_peer, y_peer)
    others = (y_peer, x_peer)
    number = {}

    def place(u, gg, dd, cols=None):
        if cols is None:
            return held.at[gg, dd] if u == 0 else fcs.at[:, gg, dd]
        return held.at[gg, dd, :, cols] if u == 0 else fcs.at[:, gg, dd, :, cols]

    def sem_of(key):
        return number.setdefault(key, len(number))

    def send(key, ref, peer):
        k = sem_of(key)
        return pltpu.make_async_remote_copy(
            src_ref=ref, dst_ref=ref, send_sem=send_sem.at[k], recv_sem=recv_sem.at[k],
            device_id=peer, device_id_type=MESH,
        )

    begun = []

    def begin(key, ref, peer):
        copy = send(key, ref, peer)
        copy.start()
        begun.append(copy)

    def arrive(key, ref, peer):
        send(key, ref, peer).wait_recv()

    def cross(u):
        for s in range(1, n_mp):
            begin(("z", u, s), place(u, g, d), (d, across[s]))

    def stage_a(u, s):
        gg = across[s]
        if s:
            arrive(("z", u, s), place(u, gg, d), (d, gg))
        for h in range(2):
            begin(("p", u, s, h), place(u, gg, d, halves[h]), (firsts[h], g))
        begin(("c", u, s, 0), place(u, gg, d), (twin, g))

    def stage_b(u, s):
        gg = across[s]
        for h in range(2):
            arrive(("p", u, s, h), place(u, gg, firsts[h], halves[h]), (firsts[h], g))
            begin(("q", u, s, h, 0), place(u, gg, d, halves[h]), (others[h], g))
            begin(("q", u, s, h, 1), place(u, gg, firsts[h], halves[h]), (others[h], g))

    def stage_c(u, s):
        gg = across[s]
        for h in range(2):
            arrive(("q", u, s, h, 0), place(u, gg, others[h], halves[h]), (others[h], g))
            arrive(("q", u, s, h, 1), place(u, gg, d ^ 6, halves[h]), (others[h], g))
        for n, dd in enumerate((x_peer, y_peer, d ^ 6)):
            begin(("c", u, s, n + 1), place(u, gg, dd), (twin, g))

    def stage_d(u, s):
        gg = across[s]
        for n, dd in enumerate((d, x_peer, y_peer, d ^ 6)):
            arrive(("c", u, s, n), place(u, gg, dd ^ 1), (twin, g))

    cross(0)
    stage_a(0, 0)
    own1.wait()
    own2.wait()
    cross(1)
    order = [(0, 0), (1, 0)] + [(0, s) for s in range(1, n_mp)] + [(1, s) for s in range(1, n_mp)]
    outs = []

    def settle():
        for s in range(n_mp):
            stage_d(0, s)

        def spread(dd, carry):
            rows = pl.ds(pl.multiple_of(dd * depth, 16), depth)
            for gg in range(n_mp):
                for j in range(3):
                    c = (j * n_mp + gg) * part
                    wqkv[rows, c : c + part] = held[gg, dd, 0:depth, j * part : (j + 1) * part]
                wproj[rows, gg * part : (gg + 1) * part] = held[gg, dd, 0:depth, 3 * part : 4 * part]
            return carry

        lax.fori_loop(0, held.shape[1], spread, 0)
        for n, (src, dst) in enumerate(((wqkv, wqkv_o), (wproj, wproj_o))):
            copy = pltpu.make_async_copy(src, dst, out_sem.at[n])
            copy.start()
            outs.append(copy)
        vec_o[...] = jnp.zeros_like(vec_o)
        qb_o[...] = jnp.zeros_like(qb_o)
        fb_o[...] = jnp.zeros_like(fb_o)
        for dd in range(held.shape[1]):
            piece = held[0, dd, depth : depth + SMALL_ROWS, :].astype(f32)
            vec_o[0:6, dd * depth : (dd + 1) * depth] = piece[0:6, 0:depth]
        for gg in range(n_mp):
            piece = held[gg, 0, depth : depth + SMALL_ROWS, :].astype(f32)
            qb_o[0:2, gg * part : (gg + 1) * part] = piece[6:8, 0:part]
            fb_o[gg : gg + 1, :] = piece[8:9, :]

    for k in range(1, len(order) + 2):
        if k < len(order):
            stage_a(*order[k])
        if k - 1 < len(order):
            stage_b(*order[k - 1])
        if 0 <= k - 2 < len(order):
            stage_c(*order[k - 2])
            if order[k - 2] == (0, n_mp - 1):
                settle()
    for s in range(n_mp):
        stage_d(1, s)
    for copy in begun:
        copy.wait_send()
    for copy in outs:
        copy.wait()


def gather_weights(qkv_w, proj_w, fc1_w, fc2_w, gains, shifts, qkv_b, fc1_b, n_dp, n_mp):
    depth, width = fc1_w.shape
    part = qkv_w.shape[2]
    transfers = 2 * (n_mp - 1) + 2 * n_mp * 10
    dma = pltpu.SemaphoreType.DMA
    outs = pl.pallas_call(
        functools.partial(gather_kernel, n_mp),
        name="gather",
        in_specs=[VMEM, VMEM, ANY, ANY, VMEM, VMEM, VMEM, VMEM],
        out_specs=[ANY, ANY, ANY, VMEM, VMEM, VMEM],
        out_shape=[
            struct((width, 3 * n_mp * part), bf16),
            struct((width, n_mp * part), bf16),
            struct((2, n_mp, n_dp, depth, width), bf16),
            struct((8, width), f32),
            struct((8, n_mp * part), f32),
            struct((8, width), f32),
        ],
        scratch_shapes=[
            pltpu.VMEM((n_mp, n_dp, depth + SMALL_ROWS, width), bf16),
            pltpu.VMEM((width, 3 * n_mp * part), bf16),
            pltpu.VMEM((width, n_mp * part), bf16),
            pltpu.VMEM((SMALL_ROWS, width), f32),
            dma((2,)),
            dma((2,)),
            dma((transfers,)),
            dma((transfers,)),
        ],
        compiler_params=pltpu.CompilerParams(
            vmem_limit_bytes=32 * 2**20, collective_id=0, has_side_effects=True
        ),
    )(qkv_w, proj_w, fc1_w, fc2_w, gains, shifts, qkv_b, fc1_b)
    wqkv, wproj, fcs, vec, qb, fb = outs
    fcs = fcs.reshape(2, n_mp, width, width)
    return wqkv, wproj, fcs, vec, qb, fb


def scatter_kernel(
    ga, small2, small3, gb, qb, main_o, small_o,
    first, c_recv, c_sum, a_out, a_recv, a_sum, b_out, b_recv, s_send, s_recv, own_sem, send_sem, recv_sem,
):
    g = lax.axis_index("mp")
    d = lax.axis_index("dp")
    y, x, c = d // 4, (d // 2) % 2, d % 2
    x_peer, y_peer, twin = d ^ 2, d ^ 4, d ^ 1
    depth, width = main_o.shape
    half = width // 2
    greet([(x_peer, g), (y_peer, g), (twin, g)])

    def send(k, src, dst, peer):
        copy = pltpu.make_async_remote_copy(
            src_ref=src, dst_ref=dst, send_sem=send_sem.at[k], recv_sem=recv_sem.at[k],
            device_id=(peer, g), device_id_type=MESH,
        )
        copy.start()
        return copy

    begun = [send(0, ga.at[:, :, 1 - c], c_recv, twin)]
    own = pltpu.make_async_copy(ga.at[:, :, c], first, own_sem.at[0])
    own.start()
    total = jnp.concatenate(
        [
            jnp.sum(v, axis=0, keepdims=True)
            for v in (small3[0], small2[0], small3[2], small3[1], small2[1], small2[2], gb[...])
        ],
        axis=0,
    )
    s_send[0, 0:7, :] = total
    s_send[0, 7:9, :] = jnp.zeros((2, width), f32)
    s_send[0, 9:16, :] = jnp.zeros((7, width), f32)
    s_send[0, 7:8, 0 : qb.shape[2]] = jnp.sum(qb[0], axis=0, keepdims=True)
    s_send[0, 8:9, 0 : qb.shape[2]] = jnp.sum(qb[1], axis=0, keepdims=True)
    begun.append(send(1, s_send.at[0], s_recv.at[0], twin))

    own.wait()
    begun[0].wait_recv()
    c_sum[...] = first[...].astype(f32) + c_recv[...].astype(f32)
    for k in range(2):
        a_out[0, k] = c_sum[k, 1 - x, :, 0:half].astype(bf16)
        a_out[1, k] = c_sum[1 - y, k, :, half:width].astype(bf16)
    begun.append(send(2, a_out.at[0], a_recv.at[0], x_peer))
    begun.append(send(3, a_out.at[1], a_recv.at[1], y_peer))
    begun[1].wait_recv()
    s_send[1] = s_send[0] + s_recv[0]
    begun.append(send(4, s_send.at[1], s_recv.at[1], x_peer))

    begun[2].wait_recv()
    for k in range(2):
        a_sum[0, k] = c_sum[k, x, :, 0:half] + a_recv[0, k].astype(f32)
    b_out[0] = a_sum[0, 1 - y].astype(bf16)
    begun.append(send(5, b_out.at[0], b_recv.at[0], y_peer))
    begun[3].wait_recv()
    for k in range(2):
        a_sum[1, k] = c_sum[y, k, :, half:width] + a_recv[1, k].astype(f32)
    b_out[1] = a_sum[1, 1 - x].astype(bf16)
    begun.append(send(6, b_out.at[1], b_recv.at[1], x_peer))
    begun[4].wait_recv()
    s_send[2] = s_send[1] + s_recv[1]
    begun.append(send(7, s_send.at[2], s_recv.at[2], y_peer))

    begun[5].wait_recv()
    main_o[:, 0:half] = a_sum[0, y] + b_recv[0].astype(f32)
    begun[6].wait_recv()
    main_o[:, half:width] = a_sum[1, x] + b_recv[1].astype(f32)
    begun[7].wait_recv()
    small_o[...] = s_send[2] + s_recv[2]
    for copy in begun:
        copy.wait_send()


def scatter_grads(ga, small2, small3, gb, qb):
    n_dp, depth, width = ga.shape
    half = width // 2
    dma = pltpu.SemaphoreType.DMA
    return pl.pallas_call(
        scatter_kernel,
        name="scatter",
        in_specs=[ANY, VMEM, VMEM, VMEM, VMEM],
        out_specs=[VMEM, VMEM],
        out_shape=[struct((depth, width), f32), struct((16, width), f32)],
        scratch_shapes=[
            pltpu.VMEM((2, 2, depth, width), bf16),
            pltpu.VMEM((2, 2, depth, width), bf16),
            pltpu.VMEM((2, 2, depth, width), f32),
            pltpu.VMEM((2, 2, depth, half), bf16),
            pltpu.VMEM((2, 2, depth, half), bf16),
            pltpu.VMEM((2, 2, depth, half), f32),
            pltpu.VMEM((2, depth, half), bf16),
            pltpu.VMEM((2, depth, half), bf16),
            pltpu.VMEM((3, 16, width), f32),
            pltpu.VMEM((3, 16, width), f32),
            dma((1,)),
            dma((8,)),
            dma((8,)),
        ],
        compiler_params=pltpu.CompilerParams(
            vmem_limit_bytes=32 * 2**20, collective_id=1, has_side_effects=True
        ),
    )(ga.reshape(2, 2, 2, depth, width), small2, small3, gb, qb)


def run_group(patches, counts, kept, cot, vec, qkv_b, fc1_b, wqkv, wproj, fcs, me, own):
    images, patch_count, width = patches.shape
    slot_count = cot.shape[1]
    inner = wproj.shape[1]
    pairs = inner // KEYS
    _, groups, _, unit = fcs.shape
    cap = -(-((images - 1) * ROWS + KEYS) // BLOCK) * BLOCK
    nmax = cap // BLOCK
    dma = pltpu.SemaphoreType.DMA
    vis, gm, qkv, att, prob, mid = pl.pallas_call(
        functools.partial(attend_kernel, images, pairs),
        name="attend",
        in_specs=[SMEM, VMEM, ANY, ANY, VMEM, VMEM, VMEM, VMEM],
        out_specs=[ANY] * 6,
        out_shape=[
            struct((cap, width), bf16),
            struct((cap, width), bf16),
            struct((cap, 3 * inner), bf16),
            struct((cap, inner), bf16),
            struct((images, ROWS, 2 * pairs * KEYS), bf16),
            struct((cap, width), f32),
        ],
        scratch_shapes=[
            pltpu.SMEM((images,), jnp.int32),
            pltpu.VMEM((images, patch_count, width), bf16),
            pltpu.VMEM((images, ROWS, width), bf16),
            pltpu.VMEM((cap, width), bf16),
            pltpu.VMEM((cap, width), bf16),
            pltpu.VMEM((cap, 3 * inner), bf16),
            pltpu.VMEM((cap, inner), bf16),
            pltpu.VMEM((images, ROWS, 2 * pairs * KEYS), bf16),
            pltpu.VMEM((cap, width), f32),
            dma((images,)),
            dma((images,)),
            dma((5, nmax)),
            dma((images,)),
        ],
        **PARAMS,
    )(counts, kept, patches, cot, wqkv, wproj, vec, qkv_b)
    out, gmid, gfc, gb, small2 = pl.pallas_call(
        functools.partial(mlp_kernel, images, groups),
        name="mlp",
        in_specs=[SMEM, SMEM, ANY, ANY, VMEM, VMEM, VMEM],
        out_specs=[ANY, ANY, VMEM, VMEM, VMEM],
        out_shape=[
            struct((images, slot_count, width), bf16),
            struct((cap, width), f32),
            struct((width, 2 * unit), bf16),
            struct((8, unit), f32),
            struct((3, 8, width), f32),
        ],
        scratch_shapes=[
            pltpu.SMEM((images,), jnp.int32),
            pltpu.VMEM((cap, width), f32),
            pltpu.VMEM((cap, width), bf16),
            pltpu.VMEM((cap, width), bf16),
            pltpu.VMEM((images, slot_count, width), bf16),
            pltpu.VMEM((2, width, unit), f32),
            dma((2, nmax)),
            dma((nmax,)),
            dma((images,)),
        ],
        **PARAMS,
    )(me, counts, mid, gm, fcs, vec, fc1_b)
    window = -(-own // KEYS) * KEYS
    pg, ga, small3, qb = pl.pallas_call(
        functools.partial(back_kernel, images, pairs),
        name="back",
        in_specs=[SMEM, SMEM, VMEM, ANY, ANY, ANY, ANY, ANY, VMEM, VMEM, VMEM],
        out_specs=[ANY, VMEM, VMEM, VMEM],
        out_shape=[
            struct((images, patch_count, width), f32),
            struct((width, 4 * own), bf16),
            struct((3, 8, width), f32),
            struct((2, 8, own), f32),
        ],
        scratch_shapes=[
            pltpu.SMEM((images,), jnp.int32),
            pltpu.VMEM((cap, width), f32),
            pltpu.VMEM((cap, 3 * inner), bf16),
            pltpu.VMEM((cap, window), bf16),
            pltpu.VMEM((2, ROWS, 2 * pairs * KEYS), bf16),
            pltpu.VMEM((cap, width), bf16),
            pltpu.VMEM((cap, inner), bf16),
            pltpu.VMEM((cap, 3 * inner), bf16),
            pltpu.VMEM((3, width, window), f32),
            pltpu.VMEM((width, window), f32),
            pltpu.VMEM((2, 8, window), f32),
            pltpu.VMEM((2, patch_count, width), f32),
            dma((4, nmax)),
            dma((2,)),
            dma((2,)),
        ],
        **PARAMS,
    )(me, counts, kept, gmid, qkv, att, prob, vis, wqkv, wproj, vec)
    return out, pg, (gfc, ga, small2, small3, gb, qb)


def per_device(
    patches,
    counts,
    kept_patches,
    cotangent,
    norm_gains,
    shifts,
    qkv_weight,
    qkv_bias,
    proj_weight,
    fc1_weight,
    fc1_bias,
    fc2_weight,
):
    image_count, patch_count, width = patches.shape
    n_mp = lax.axis_size("mp")
    me = lax.axis_index("mp").astype(jnp.int32).reshape(1)
    own = qkv_weight.shape[2]
    inner = own * n_mp

    n_dp = lax.axis_size("dp")
    depth = width // n_dp
    direct = n_dp == 8 and n_mp == 4 and depth % 16 == 0
    if direct:
        wqkv, wproj, fcs, vec, qkv_b, fc1_b = gather_weights(
            qkv_weight.transpose(1, 0, 2), proj_weight, fc1_weight, fc2_weight.T,
            norm_gains, shifts, qkv_bias, fc1_bias.reshape(1, -1), n_dp, n_mp,
        )
    else:
        vec = lax.all_gather(jnp.concatenate([norm_gains, shifts]), "dp", axis=1, tiled=True)
        vec = jnp.pad(vec.astype(f32), ((0, 2), (0, 0)))
        wqkv = lax.all_gather(lax.all_gather(qkv_weight, "mp", axis=2, tiled=True), "dp", axis=0, tiled=True)
        wqkv = wqkv.reshape(width, 3 * inner)
        qkv_b = lax.all_gather(qkv_bias, "mp", axis=1, tiled=True).astype(f32)
        wproj = lax.all_gather(lax.all_gather(proj_weight.T, "mp", axis=1, tiled=True), "dp", axis=0, tiled=True)
        both = jnp.stack([fc1_weight, fc2_weight.T])
        fcs = lax.all_gather(lax.all_gather(both, "mp", axis=1), "dp", axis=2, tiled=True)
        fc1_b = lax.all_gather(fc1_bias, "mp", axis=0).astype(f32)

    group = max(n for n in range(1, GROUP_MAX + 1) if image_count % n == 0)
    outs, pgs, grads = [], [], []
    for first in range(0, image_count, group):
        part = slice(first, first + group)
        out, pg, grad = run_group(
            patches[part], counts[part], kept_patches[part], cotangent[part],
            vec, qkv_b, fc1_b, wqkv, wproj, fcs, me, own,
        )
        outs.append(out)
        pgs.append(pg)
        grads.append(grad)
    if len(grads) > 1:
        grads = [tuple(sum(item.astype(f32) for item in items) for items in zip(*grads))]
    gfc, ga, small2, small3, gb, qb = grads[0]
    hid = fc1_weight.shape[1]
    gfc = lax.psum_scatter(gfc.astype(bf16), "dp", scatter_dimension=0, tiled=True).astype(f32)
    if direct:
        main, small = scatter_grads(ga.astype(bf16).reshape(n_dp, depth, -1), small2, small3, gb, qb)
    else:
        main = lax.psum_scatter(ga.astype(bf16), "dp", scatter_dimension=0, tiled=True).astype(f32)
        rows = [small3[0], small2[0], small3[2], small3[1], small2[1], small2[2], gb]
        rows += [jnp.pad(qb[n], ((0, 0), (0, width - own))) for n in range(2)]
        small = lax.psum(jnp.stack([jnp.sum(row, axis=0) for row in rows]), "dp")
    mine = lax.dynamic_slice_in_dim(small[:6], lax.axis_index("dp") * depth, depth, 1)
    return (
        outs[0] if len(outs) == 1 else jnp.concatenate(outs, axis=0),
        pgs[0] if len(pgs) == 1 else jnp.concatenate(pgs, axis=0),
        mine[:2],
        mine[2:],
        jnp.stack([main[:, j * own : (j + 1) * own] for j in range(3)]).transpose(1, 0, 2),
        small[7:9, :own],
        main[:, 3 * own : 4 * own].T,
        gfc[:, :hid],
        small[6],
        gfc[:, hid:].T,
    )


def solution(mesh):
    placed = (
        P("dp", None, None),
        P("dp"),
        P("dp", None),
        P("dp", None, None),
        P(None, "dp"),
        P(None, "dp"),
        P("dp", None, "mp"),
        P(None, "mp"),
        P("mp", "dp"),
        P("dp", "mp"),
        P("mp"),
        P("mp", "dp"),
    )
    return jax.shard_map(
        per_device,
        mesh=mesh,
        in_specs=placed,
        out_specs=(
            P("dp", None, None),
            P("dp", None, None),
            P(None, "dp"),
            P(None, "dp"),
            P("dp", None, "mp"),
            P(None, "mp"),
            P("mp", "dp"),
            P("dp", "mp"),
            P("mp"),
            P("mp", "dp"),
        ),
        check_vma=False,
    )
```

```python
import functools

import jax
import jax.numpy as jnp
from jax import lax
from jax.experimental import pallas as pl
from jax.experimental.pallas import tpu as pltpu
from jax.sharding import PartitionSpec as P

HD = 64
KEEP_MAX = 98
ROWS = 112
ROW_CHOICES = (64, 80, 96, 112)
KEYS = 128
BLOCK = 256
PAIRS_AT_ONCE = 6
GROUP_MAX = 24
EPSILON = 1e-06
VMEM_BYTES = 59 * 2**20

f32 = jnp.float32
bf16 = jnp.bfloat16

NN = (((1,), (0,)), ((), ()))
NT = (((1,), (1,)), ((), ()))
TN = (((0,), (0,)), ((), ()))


def dot(left, right, dims=NN):
    return lax.dot_general(left, right, dims, preferred_element_type=f32)


def norm_stats(values):
    row_mean = jnp.mean(values, axis=-1, keepdims=True)
    centred = values - row_mean
    inverse = lax.rsqrt(jnp.mean(centred * centred, axis=-1, keepdims=True) + EPSILON)
    return centred * inverse, inverse


def norm_pull(grad_normed, normed, inverse, gain_row):
    scaled = grad_normed * gain_row
    first_mean = jnp.mean(scaled, axis=-1, keepdims=True)
    second_mean = jnp.mean(scaled * normed, axis=-1, keepdims=True)
    return inverse * (scaled - first_mean - normed * second_mean)


def fold_rows(values):
    rows, width = values.shape
    return jnp.sum(values.reshape(rows // 8, 8, width), axis=0)


def gelu_parts(u):
    bell = jnp.exp(u * u * -0.5)
    t = 1.0 / (1.0 + 0.23164190 * jnp.abs(u))
    poly = 0.5307027145
    for c in (-0.7265760135, 0.7107068705, -0.142248368, 0.127414796):
        poly = poly * t + c
    tail = poly * t * bell
    cdf = jnp.where(u >= 0, 1.0 - tail, tail)
    return u * cdf, cdf + u * bell * 0.3989422804014327


def fill_offsets(counts, offs, images):
    def step(i, total):
        offs[i] = total
        return total + lax.div(counts[i] + 15, 16) * 16

    total = lax.fori_loop(0, images, step, 0)
    return lax.div(total + BLOCK - 1, BLOCK)


def lane_split(values):
    left = lax.broadcasted_iota(jnp.int32, values.shape, 1) < HD
    zero = jnp.zeros_like(values)
    return jnp.concatenate([jnp.where(left, values, zero), jnp.where(left, zero, values)], axis=0)


def head_marks():
    shape = (2 * KEYS, KEYS)
    first = lax.broadcasted_iota(jnp.int32, shape, 0) < KEYS
    left = lax.broadcasted_iota(jnp.int32, shape, 1) < HD
    return jnp.where(first == left, 1.0, 0.0).astype(bf16)


def with_marks(values):
    return jnp.concatenate([lane_split(values), head_marks()], axis=1)


def row_block(b):
    return pl.ds(pl.multiple_of(b * BLOCK, BLOCK), BLOCK)


def by_rows(count, body):
    low = 0
    for rows in ROW_CHOICES:
        @pl.when((count > low) & (count <= rows))
        def _(rows=rows):
            body(rows)

        low = rows


def attend_kernel(
    images, pairs, counts, kept, patches, cot, wqkv, wproj, vec, bias,
    vis_o, gm_o, qkv_o, att_o, mid_o,
    offs, pbuf, cbuf, wqkv_v, wproj_v, vis, gm, qkv, att, mid,
    in_sem, cot_sem, blk_sem, w_sem,
):
    width = vis.shape[1]
    inner = att.shape[1]
    nblk = fill_offsets(counts, offs, images)

    def patch_copy(i):
        return pltpu.make_async_copy(patches.at[i], pbuf.at[i], in_sem.at[i])

    def cot_copy(i):
        return pltpu.make_async_copy(cot.at[i, pl.ds(0, ROWS)], cbuf.at[i], cot_sem.at[i])

    def start_in(i, carry):
        patch_copy(i).start()
        cot_copy(i).start()
        return carry

    lax.fori_loop(0, images, start_in, 0)
    load_qkv = pltpu.make_async_copy(wqkv, wqkv_v, w_sem.at[0])
    load_proj = pltpu.make_async_copy(wproj, wproj_v, w_sem.at[1])
    load_qkv.start()
    load_proj.start()

    def clear(b, carry):
        rows = row_block(b)
        vis[rows, :] = jnp.zeros((BLOCK, width), bf16)
        gm[rows, :] = jnp.zeros((BLOCK, width), bf16)
        att[rows, :] = jnp.zeros((BLOCK, inner), bf16)
        return carry

    lax.fori_loop(0, nblk, clear, 0)
    after = pl.ds(pl.multiple_of(nblk * BLOCK, BLOCK), KEYS)
    qkv[after, :] = jnp.zeros((KEYS, qkv.shape[1]), bf16)

    def gather(i, carry):
        patch_copy(i).wait()
        cot_copy(i).wait()
        off = pl.multiple_of(offs[i], 16)
        kept_row = kept[pl.ds(i, 1), :]
        patch_ids = lax.broadcasted_iota(jnp.int32, (pbuf.shape[1], KEYS), 0)
        onehot = jnp.where(patch_ids == kept_row, 1.0, 0.0).astype(bf16)
        vis[pl.ds(off, KEYS), :] = dot(onehot, pbuf[i], TN).astype(bf16)
        live = lax.broadcasted_iota(jnp.int32, (ROWS, width), 0) < counts[i]
        gm[pl.ds(off, ROWS), :] = jnp.where(live, cbuf[i], jnp.zeros((ROWS, width), bf16))
        return carry

    lax.fori_loop(0, images, gather, 0)

    def out_copies(b, which=(0, 1, 2, 3, 4)):
        rows = row_block(b)
        pairs_of = ((vis, vis_o), (gm, gm_o), (qkv, qkv_o), (att, att_o), (mid, mid_o))
        return [
            pltpu.make_async_copy(pairs_of[n][0].at[rows], pairs_of[n][1].at[rows], blk_sem.at[n, b])
            for n in which
        ]

    def project(b, carry):
        rows = row_block(b)
        normed, _ = norm_stats(vis[rows, :].astype(f32))
        source = (normed * vec[0:1, :] + vec[2:3, :]).astype(bf16)
        for j in range(3):
            cols = slice(j * inner, (j + 1) * inner)
            part = dot(source, wqkv_v[:, cols])
            if j == 0:
                part = (part + bias[0:1, :]) * (HD**-0.5)
            if j == 2:
                part = part + bias[1:2, :]
            qkv[rows, cols] = part.astype(bf16)
        for copy in out_copies(b, (0, 1, 2)):
            copy.start()
        return carry

    load_qkv.wait()
    lax.fori_loop(0, nblk, project, 0)

    def attend(i, carry):
        off = pl.multiple_of(offs[i], 16)
        count = counts[i]

        def body(rows):
            key_live = lax.broadcasted_iota(jnp.int32, (rows, KEYS), 1) < count
            held = []
            for p in range(pairs):
                c = p * KEYS
                q2 = qkv[pl.ds(off, rows), c : c + KEYS]
                k2 = qkv[pl.ds(off, KEYS), inner + c : inner + c + KEYS]
                v2 = qkv[pl.ds(off, KEYS), 2 * inner + c : 2 * inner + c + KEYS]
                held.append((c, v2, dot(q2, lane_split(k2), NT)))
            ready = []
            for c, v2, scores in held:
                halves = []
                for h in range(2):
                    s = jnp.where(key_live, scores[:, h * KEYS : (h + 1) * KEYS], -1e30)
                    halves.append(jnp.exp(s - jnp.max(s, axis=-1, keepdims=True)).astype(bf16))
                ready.append((c, v2, jnp.concatenate(halves, axis=1)))
            done = [(c, dot(ex, with_marks(v2))) for c, v2, ex in ready]
            for c, both in done:
                att[pl.ds(off, rows), c : c + KEYS] = (both[:, :KEYS] / both[:, KEYS:]).astype(bf16)

        by_rows(count, body)
        return carry

    lax.fori_loop(0, images, attend, 0)
    load_proj.wait()

    def finish(b, carry):
        rows = row_block(b)
        attention = dot(att[rows, :], wproj_v[...], NT) + vec[3:4, :]
        mid[rows, :] = vis[rows, :].astype(f32) + attention
        for copy in out_copies(b, (3, 4)):
            copy.start()
        return carry

    lax.fori_loop(0, nblk, finish, 0)

    def drain(b, carry):
        for copy in out_copies(b):
            copy.wait()
        return carry

    lax.fori_loop(0, nblk, drain, 0)


def mlp_kernel(
    images, groups, me_ref, counts, mid_h, gm_h, fcs, vec, bias,
    out_o, gmid_o, gfc_o, gb_o, small_o,
    offs, mid, gm, out, stage, acc, fcv, in_sem, gmid_sem, out_sem, w_sem,
):
    width = mid.shape[1]
    me = me_ref[0]
    nblk = fill_offsets(counts, offs, images)

    def in_copies(b):
        rows = row_block(b)
        return (
            pltpu.make_async_copy(mid_h.at[rows], mid.at[rows], in_sem.at[0, b]),
            pltpu.make_async_copy(gm_h.at[rows], gm.at[rows], in_sem.at[1, b]),
        )

    def start_in(b, carry):
        for copy in in_copies(b):
            copy.start()
        return carry

    lax.fori_loop(0, nblk, start_in, 0)

    def load(s):
        g = lax.rem(me + s, groups)
        return pltpu.make_async_copy(fcs.at[:, g], fcv.at[s], w_sem.at[s])

    for s in range(groups):
        load(s).start()
    acc[...] = jnp.zeros_like(acc)
    gb_o[...] = jnp.zeros_like(gb_o)
    small_o[...] = jnp.zeros_like(small_o)

    def gmid_copy(b):
        rows = row_block(b)
        return pltpu.make_async_copy(mid.at[rows], gmid_o.at[rows], gmid_sem.at[b])

    def block(b, carry):
        rows = row_block(b)
        for copy in in_copies(b):
            copy.wait()
        normed, inverse = norm_stats(mid[rows, :])
        source = (normed * vec[1:2, :] + vec[4:5, :]).astype(bf16)
        gmb = gm[rows, :]
        sums = [None, None]
        opened, kept_back = {}, {}

        def open_group(s):
            g = lax.rem(me + s, groups)
            pre = dot(source, fcv[s, 0]) + bias[pl.ds(g, 1), :]
            opened[s] = (pre, dot(gmb, fcv[s, 1]))

        def close_group(s):
            pre, grad_act = opened.pop(s)
            act, slope = gelu_parts(pre)
            act = act.astype(bf16)
            gp = (grad_act * slope).astype(bf16)
            parts = (dot(act, fcv[s, 1], NT), dot(gp, fcv[s, 0], NT))
            for n in range(2):
                sums[n] = parts[n] if sums[n] is None else sums[n] + parts[n]
            if s == 0:
                kept_back["own"] = (act, gp)

        open_group(0)
        for s in range(groups):
            if s + 1 < groups:
                open_group(s + 1)
            close_group(s)
        mlp, gnm = sums
        act, gp = kept_back["own"]
        acc[0] += dot(source, gp, TN)
        acc[1] += dot(gmb, act, TN)
        gb_o[...] += fold_rows(gp.astype(f32))
        out[rows, :] = (mid[rows, :] + mlp + vec[5:6, :]).astype(bf16)
        grad_mid = gmb.astype(f32) + norm_pull(gnm, normed, inverse, vec[1:2, :])
        small_o[0] += fold_rows(gnm * normed)
        small_o[1] += fold_rows(gnm)
        small_o[2] += fold_rows(gmb.astype(f32))
        mid[rows, :] = grad_mid
        gmid_copy(b).start()
        return carry

    for s in range(groups):
        load(s).wait()
    lax.fori_loop(0, nblk, block, 0)
    for n in range(2):
        gfc_o[:, n * acc.shape[2] : (n + 1) * acc.shape[2]] = acc[n].astype(bf16)

    def out_copy(i):
        return pltpu.make_async_copy(stage.at[i], out_o.at[i], out_sem.at[i])

    def unpack(i, carry):
        off = pl.multiple_of(offs[i], 16)
        slots = stage.shape[1]
        live = lax.broadcasted_iota(jnp.int32, (ROWS, width), 0) < counts[i]
        stage[i, pl.ds(0, ROWS), :] = jnp.where(live, out[pl.ds(off, ROWS), :], jnp.zeros((ROWS, width), bf16))
        if slots > ROWS:
            stage[i, pl.ds(ROWS, slots - ROWS), :] = jnp.zeros((slots - ROWS, width), bf16)
        out_copy(i).start()
        return carry

    lax.fori_loop(0, images, unpack, 0)

    def drain(i, carry):
        out_copy(i).wait()
        return carry

    lax.fori_loop(0, images, drain, 0)

    def drain_gmid(b, carry):
        gmid_copy(b).wait()
        return carry

    lax.fori_loop(0, nblk, drain_gmid, 0)


def back_kernel(
    images, pairs, me_ref, counts, kept, gmid_h, qkv_h, att_h, vis_h, wqkv, wproj, vec,
    pg_o, ga_o, small_o, qb_o,
    offs, gmid, qkv, att, vis, gat, dqkv, accq, accp, qsum, stage, wqkv_v, wproj_v,
    in_sem, pg_sem, w_sem, gmid_sem,
):
    width = vis.shape[1]
    inner = gat.shape[1]
    me = me_ref[0]
    own = qb_o.shape[2]
    window = accp.shape[1]
    start = pl.multiple_of(lax.div(me * own, KEYS) * KEYS, KEYS)
    nblk = fill_offsets(counts, offs, images)

    def in_copies(b, which=(0, 1, 2)):
        rows = row_block(b)
        pairs_of = (
            (att_h.at[rows, pl.ds(start, window)], att),
            (qkv_h.at[rows], qkv),
            (vis_h.at[rows], vis),
        )
        return [
            pltpu.make_async_copy(pairs_of[n][0], pairs_of[n][1].at[rows], in_sem.at[n, b])
            for n in which
        ]

    load_proj = pltpu.make_async_copy(wproj, wproj_v, w_sem.at[0])
    load_qkv = pltpu.make_async_copy(wqkv, wqkv_v, w_sem.at[1])
    load_proj.start()
    depth = gmid.shape[0]

    def gmid_copy(b):
        slot = lax.rem(b, depth)
        return pltpu.make_async_copy(gmid_h.at[row_block(b)], gmid.at[slot], gmid_sem.at[slot])

    def gmid_begin():
        for b in range(depth - 1):
            @pl.when(b < nblk)
            def _(b=b):
                gmid_copy(b).start()

    def gmid_block(b):
        gmid_copy(b).wait()

        @pl.when(b + depth - 1 < nblk)
        def _():
            gmid_copy(b + depth - 1).start()

        return gmid[lax.rem(b, depth)]

    gmid_begin()

    def start_first(b, carry):
        for copy in in_copies(b, (0,)):
            copy.start()
        return carry

    def start_rest(b, carry):
        for copy in in_copies(b, (1, 2)):
            copy.start()
        return carry

    lax.fori_loop(0, nblk, start_first, 0)
    lax.fori_loop(0, nblk, start_rest, 0)
    load_qkv.start()
    accq[...] = jnp.zeros_like(accq)
    accp[...] = jnp.zeros_like(accp)
    small_o[...] = jnp.zeros_like(small_o)
    qsum[...] = jnp.zeros_like(qsum)

    def first(b, carry):
        rows = row_block(b)
        for copy in in_copies(b, (0,)):
            copy.wait()
        ga = gmid_block(b).astype(bf16)
        small_o[1] += fold_rows(ga.astype(f32))
        gat[rows, :] = dot(ga, wproj_v[...]).astype(bf16)
        accp[...] += dot(ga, att[rows, :], TN)
        dqkv[rows, :] = jnp.zeros((BLOCK, dqkv.shape[1]), bf16)
        return carry

    load_proj.wait()
    lax.fori_loop(0, nblk, first, 0)
    after = pl.ds(pl.multiple_of(nblk * BLOCK, BLOCK), KEYS)
    qkv[after, :] = jnp.zeros((KEYS, qkv.shape[1]), bf16)
    gat[after, :] = jnp.zeros((KEYS, inner), bf16)

    def wait_rest(b, carry):
        for copy in in_copies(b, (1, 2)):
            copy.wait()
        return carry

    lax.fori_loop(0, nblk, wait_rest, 0)

    gmid_begin()

    def attend(i, carry):
        off = pl.multiple_of(offs[i], 16)
        count = counts[i]
        left = lax.broadcasted_iota(jnp.int32, (KEYS, KEYS), 1) < HD
        row_live = lax.broadcasted_iota(jnp.int32, (KEYS, KEYS), 0) < count
        square = (KEYS, KEYS)
        eye = jnp.where(
            lax.broadcasted_iota(jnp.int32, square, 0) == lax.broadcasted_iota(jnp.int32, square, 1), 1.0, 0.0
        ).astype(bf16)

        def body(rows):
            key_live = lax.broadcasted_iota(jnp.int32, (rows, 2 * KEYS), 0) < count
            here = pl.ds(off, rows)
            wide = pl.ds(off, KEYS)
            for first in range(0, pairs, PAIRS_AT_ONCE):
                held = []
                for p in range(first, min(first + PAIRS_AT_ONCE, pairs)):
                    c = p * KEYS
                    qs = lane_split(qkv[wide, c : c + KEYS])
                    k2 = qkv[here, inner + c : inner + c + KEYS]
                    v2 = qkv[here, 2 * inner + c : 2 * inner + c + KEYS]
                    do2 = gat[wide, c : c + KEYS]
                    ds = lane_split(jnp.where(row_live, do2, jnp.zeros_like(do2)))
                    held.append((c, qs, k2, ds, dot(k2, qs, NT), dot(v2, ds, NT)))
                ready = []
                for c, qs, k2, ds, st, slope in held:
                    st = jnp.where(key_live, st, -1e30)
                    e = jnp.exp(st - jnp.max(st, axis=0, keepdims=True))
                    pr = e * (1.0 / jnp.sum(e, axis=0, keepdims=True))
                    delta = jnp.sum(pr * slope, axis=0, keepdims=True)
                    gs = (pr * (slope - delta)).astype(bf16)
                    ready.append((c, qs, k2, ds, pr.astype(bf16), gs))
                done = []
                for c, qs, k2, ds, pr, gs in ready:
                    dq_a = dot(gs[:, :KEYS], k2, TN)
                    dq_b = dot(gs[:, KEYS:], k2, TN)
                    dq = jnp.where(left, dq_a, dq_b)[:rows] * (HD**-0.5)
                    done.append((c, dq, dot(gs, qs), dot(pr, ds)))
                for c, dq, dk, dv in done:
                    dqkv[here, c : c + KEYS] = dq.astype(bf16)
                    dqkv[here, inner + c : inner + c + KEYS] = dk.astype(bf16)
                    dqkv[here, 2 * inner + c : 2 * inner + c + KEYS] = dv.astype(bf16)

        by_rows(count, body)
        return carry

    lax.fori_loop(0, images, attend, 0)

    def second(b, carry):
        rows = row_block(b)
        normed, inverse = norm_stats(vis[rows, :].astype(f32))
        source = (normed * vec[0:1, :] + vec[2:3, :]).astype(bf16)
        gni = dot(dqkv[rows, :], wqkv_v[...], NT)
        small_o[0] += fold_rows(gni * normed)
        small_o[2] += fold_rows(gni)
        mine = jnp.concatenate(
            [dqkv[rows, pl.ds(pl.multiple_of(j * inner + start, KEYS), window)] for j in range(3)], axis=1
        )
        accq[...] += dot(source, mine, TN)
        qsum[0] += fold_rows(mine[:, :window].astype(f32))
        qsum[1] += fold_rows(mine[:, 2 * window :].astype(f32))
        grad = gmid_block(b) + norm_pull(gni, normed, inverse, vec[0:1, :])
        gat[rows, :] = grad.astype(bf16)
        return carry

    load_qkv.wait()
    lax.fori_loop(0, nblk, second, 0)

    slots = stage.shape[0]

    def pg_copy(i):
        slot = lax.rem(i, slots)
        return pltpu.make_async_copy(stage.at[slot], pg_o.at[:, i], pg_sem.at[slot])

    def scatter(i, carry):
        @pl.when(i >= slots)
        def _():
            pg_copy(i - slots).wait()

        off = pl.multiple_of(offs[i], 16)
        kept_row = kept[pl.ds(i, 1), :]
        shape = (stage.shape[1], KEYS)
        hit = (lax.broadcasted_iota(jnp.int32, shape, 0) == kept_row) & (
            lax.broadcasted_iota(jnp.int32, shape, 1) < counts[i]
        )
        onehot = jnp.where(hit, 1.0, 0.0).astype(bf16)
        stage[lax.rem(i, slots)] = dot(onehot, gat[pl.ds(off, KEYS), :])
        pg_copy(i).start()
        return carry

    lax.fori_loop(0, images, scatter, 0)

    def drain(i, carry):
        pg_copy(i).wait()
        return carry

    lax.fori_loop(max(0, images - slots), images, drain, 0)

    def emit(shift):
        ga_o[:, 3 * own : 4 * own] = accp[:, shift : shift + own].astype(bf16)
        for j in range(3):
            ga_o[:, j * own : (j + 1) * own] = accq[:, j * window + shift : j * window + shift + own].astype(bf16)
        for n in range(2):
            qb_o[n] = qsum[n, :, shift : shift + own]

    shift = me * own - start

    @pl.when(shift == 0)
    def _():
        emit(0)

    @pl.when(shift != 0)
    def _():
        emit(window - own)


SMEM = pl.BlockSpec(memory_space=pltpu.SMEM)
VMEM = pl.BlockSpec(memory_space=pltpu.VMEM)
ANY = pl.BlockSpec(memory_space=pltpu.HBM)
PARAMS = dict(compiler_params=pltpu.CompilerParams(vmem_limit_bytes=VMEM_BYTES))


def struct(shape, dtype):
    return jax.ShapeDtypeStruct(shape, dtype)


MESH = pl.DeviceIdType.MESH
SMALL_ROWS = 16


def greet(peers):
    barrier = pltpu.get_barrier_semaphore()
    for peer in peers:
        pl.semaphore_signal(barrier, inc=1, device_id=peer, device_id_type=MESH)
    pl.semaphore_wait(barrier, len(peers))


def gather_kernel(
    n_mp, qkv_w, proj_w, fc1_w, fc2_w, gains, shifts, qkv_b, fc1_b,
    wqkv_o, wproj_o, fcs, vec_o, qb_o, fb_o,
    held, wqkv, wproj, notes, own_sem, out_sem, send_sem, recv_sem,
):
    g = lax.axis_index("mp")
    d = lax.axis_index("dp")
    depth, width = fc1_w.shape
    part = qkv_w.shape[2]
    x_peer, y_peer, twin = d ^ 2, d ^ 4, d ^ 1
    across = [g ^ s for s in range(n_mp)]
    greet(
        [(d, across[s]) for s in range(1, n_mp)] + [(x_peer, g), (y_peer, g), (twin, g)]
    )
    own1 = pltpu.make_async_copy(fc1_w, fcs.at[0, g, d], own_sem.at[0])
    own2 = pltpu.make_async_copy(fc2_w, fcs.at[1, g, d], own_sem.at[1])
    own1.start()
    own2.start()
    for j in range(3):
        held[g, d, 0:depth, j * part : (j + 1) * part] = qkv_w[j]
    held[g, d, 0:depth, 3 * part : 4 * part] = proj_w[...].astype(f32).T.astype(bf16)
    notes[...] = jnp.zeros_like(notes)
    notes[0:2, 0:depth] = gains[...].astype(f32)
    notes[2:6, 0:depth] = shifts[...].astype(f32)
    notes[6:8, 0:part] = qkv_b[...].astype(f32)
    notes[8:9, :] = fc1_b[...].astype(f32)
    held[g, d, depth : depth + SMALL_ROWS, :] = notes[...].astype(bf16)

    half = width // 2
    halves = (slice(0, half), slice(half, width))
    firsts = (x_peer, y_peer)
    others = (y_peer, x_peer)
    number = {}

    def place(u, gg, dd, cols=None):
        if cols is None:
            return held.at[gg, dd] if u == 0 else fcs.at[:, gg, dd]
        return held.at[gg, dd, :, cols] if u == 0 else fcs.at[:, gg, dd, :, cols]

    def sem_of(key):
        return number.setdefault(key, len(number))

    def send(key, ref, peer):
        k = sem_of(key)
        return pltpu.make_async_remote_copy(
            src_ref=ref, dst_ref=ref, send_sem=send_sem.at[k], recv_sem=recv_sem.at[k],
            device_id=peer, device_id_type=MESH,
        )

    begun = []

    def begin(key, ref, peer):
        copy = send(key, ref, peer)
        copy.start()
        begun.append(copy)

    def arrive(key, ref, peer):
        send(key, ref, peer).wait_recv()

    def cross(u):
        for s in range(1, n_mp):
            begin(("z", u, s), place(u, g, d), (d, across[s]))

    def stage_a(u, s):
        gg = across[s]
        if s:
            arrive(("z", u, s), place(u, gg, d), (d, gg))
        for h in range(2):
            begin(("p", u, s, h), place(u, gg, d, halves[h]), (firsts[h], g))
        begin(("c", u, s, 0), place(u, gg, d), (twin, g))

    def stage_b(u, s):
        gg = across[s]
        for h in range(2):
            arrive(("p", u, s, h), place(u, gg, firsts[h], halves[h]), (firsts[h], g))
            begin(("q", u, s, h, 0), place(u, gg, d, halves[h]), (others[h], g))
            begin(("q", u, s, h, 1), place(u, gg, firsts[h], halves[h]), (others[h], g))

    def stage_c(u, s):
        gg = across[s]
        for h in range(2):
            arrive(("q", u, s, h, 0), place(u, gg, others[h], halves[h]), (others[h], g))
            arrive(("q", u, s, h, 1), place(u, gg, d ^ 6, halves[h]), (others[h], g))
        for n, dd in enumerate((x_peer, y_peer, d ^ 6)):
            begin(("c", u, s, n + 1), place(u, gg, dd), (twin, g))

    def stage_d(u, s):
        gg = across[s]
        for n, dd in enumerate((d, x_peer, y_peer, d ^ 6)):
            arrive(("c", u, s, n), place(u, gg, dd ^ 1), (twin, g))

    cross(0)
    stage_a(0, 0)
    own1.wait()
    own2.wait()
    cross(1)
    order = [(0, 0), (1, 0)] + [(0, s) for s in range(1, n_mp)] + [(1, s) for s in range(1, n_mp)]
    outs = []

    def settle():
        for s in range(n_mp):
            stage_d(0, s)

        def spread(dd, carry):
            rows = pl.ds(pl.multiple_of(dd * depth, 16), depth)
            for gg in range(n_mp):
                for j in range(3):
                    c = (j * n_mp + gg) * part
                    wqkv[rows, c : c + part] = held[gg, dd, 0:depth, j * part : (j + 1) * part]
                wproj[rows, gg * part : (gg + 1) * part] = held[gg, dd, 0:depth, 3 * part : 4 * part]
            return carry

        lax.fori_loop(0, held.shape[1], spread, 0)
        for n, (src, dst) in enumerate(((wqkv, wqkv_o), (wproj, wproj_o))):
            copy = pltpu.make_async_copy(src, dst, out_sem.at[n])
            copy.start()
            outs.append(copy)
        vec_o[...] = jnp.zeros_like(vec_o)
        qb_o[...] = jnp.zeros_like(qb_o)
        fb_o[...] = jnp.zeros_like(fb_o)
        for dd in range(held.shape[1]):
            piece = held[0, dd, depth : depth + SMALL_ROWS, :].astype(f32)
            vec_o[0:6, dd * depth : (dd + 1) * depth] = piece[0:6, 0:depth]
        for gg in range(n_mp):
            piece = held[gg, 0, depth : depth + SMALL_ROWS, :].astype(f32)
            qb_o[0:2, gg * part : (gg + 1) * part] = piece[6:8, 0:part]
            fb_o[gg : gg + 1, :] = piece[8:9, :]

    for k in range(1, len(order) + 2):
        if k < len(order):
            stage_a(*order[k])
        if k - 1 < len(order):
            stage_b(*order[k - 1])
        if 0 <= k - 2 < len(order):
            stage_c(*order[k - 2])
            if order[k - 2] == (0, n_mp - 1):
                settle()
    for s in range(n_mp):
        stage_d(1, s)
    for copy in begun:
        copy.wait_send()
    for copy in outs:
        copy.wait()


def gather_weights(qkv_w, proj_w, fc1_w, fc2_w, gains, shifts, qkv_b, fc1_b, n_dp, n_mp):
    depth, width = fc1_w.shape
    part = qkv_w.shape[2]
    transfers = 2 * (n_mp - 1) + 2 * n_mp * 10
    dma = pltpu.SemaphoreType.DMA
    outs = pl.pallas_call(
        functools.partial(gather_kernel, n_mp),
        name="gather",
        in_specs=[VMEM, VMEM, ANY, ANY, VMEM, VMEM, VMEM, VMEM],
        out_specs=[ANY, ANY, ANY, VMEM, VMEM, VMEM],
        out_shape=[
            struct((width, 3 * n_mp * part), bf16),
            struct((width, n_mp * part), bf16),
            struct((2, n_mp, n_dp, depth, width), bf16),
            struct((8, width), f32),
            struct((8, n_mp * part), f32),
            struct((8, width), f32),
        ],
        scratch_shapes=[
            pltpu.VMEM((n_mp, n_dp, depth + SMALL_ROWS, width), bf16),
            pltpu.VMEM((width, 3 * n_mp * part), bf16),
            pltpu.VMEM((width, n_mp * part), bf16),
            pltpu.VMEM((SMALL_ROWS, width), f32),
            dma((2,)),
            dma((2,)),
            dma((transfers,)),
            dma((transfers,)),
        ],
        compiler_params=pltpu.CompilerParams(
            vmem_limit_bytes=32 * 2**20, collective_id=0, has_side_effects=True
        ),
    )(qkv_w, proj_w, fc1_w, fc2_w, gains, shifts, qkv_b, fc1_b)
    wqkv, wproj, fcs, vec, qb, fb = outs
    fcs = fcs.reshape(2, n_mp, width, width)
    return wqkv, wproj, fcs, vec, qb, fb


def scatter_kernel(
    ga, small2, small3, gb, qb, main_o, small_o,
    first, c_recv, c_sum, a_out, a_recv, a_sum, b_out, b_recv, s_send, s_recv, own_sem, send_sem, recv_sem,
):
    g = lax.axis_index("mp")
    d = lax.axis_index("dp")
    y, x, c = d // 4, (d // 2) % 2, d % 2
    x_peer, y_peer, twin = d ^ 2, d ^ 4, d ^ 1
    depth, width = main_o.shape
    half = width // 2
    greet([(x_peer, g), (y_peer, g), (twin, g)])

    def send(k, src, dst, peer):
        copy = pltpu.make_async_remote_copy(
            src_ref=src, dst_ref=dst, send_sem=send_sem.at[k], recv_sem=recv_sem.at[k],
            device_id=(peer, g), device_id_type=MESH,
        )
        copy.start()
        return copy

    begun = [send(0, ga.at[:, :, 1 - c], c_recv, twin)]
    own = pltpu.make_async_copy(ga.at[:, :, c], first, own_sem.at[0])
    own.start()
    total = jnp.concatenate(
        [
            jnp.sum(v, axis=0, keepdims=True)
            for v in (small3[0], small2[0], small3[2], small3[1], small2[1], small2[2], gb[...])
        ],
        axis=0,
    )
    s_send[0, 0:7, :] = total
    s_send[0, 7:9, :] = jnp.zeros((2, width), f32)
    s_send[0, 9:16, :] = jnp.zeros((7, width), f32)
    s_send[0, 7:8, 0 : qb.shape[2]] = jnp.sum(qb[0], axis=0, keepdims=True)
    s_send[0, 8:9, 0 : qb.shape[2]] = jnp.sum(qb[1], axis=0, keepdims=True)
    begun.append(send(1, s_send.at[0], s_recv.at[0], twin))

    own.wait()
    begun[0].wait_recv()
    c_sum[...] = first[...].astype(f32) + c_recv[...].astype(f32)
    for k in range(2):
        a_out[0, k] = c_sum[k, 1 - x, :, 0:half].astype(bf16)
        a_out[1, k] = c_sum[1 - y, k, :, half:width].astype(bf16)
    begun.append(send(2, a_out.at[0], a_recv.at[0], x_peer))
    begun.append(send(3, a_out.at[1], a_recv.at[1], y_peer))
    begun[1].wait_recv()
    s_send[1] = s_send[0] + s_recv[0]
    begun.append(send(4, s_send.at[1], s_recv.at[1], x_peer))

    begun[2].wait_recv()
    for k in range(2):
        a_sum[0, k] = c_sum[k, x, :, 0:half] + a_recv[0, k].astype(f32)
    b_out[0] = a_sum[0, 1 - y].astype(bf16)
    begun.append(send(5, b_out.at[0], b_recv.at[0], y_peer))
    begun[3].wait_recv()
    for k in range(2):
        a_sum[1, k] = c_sum[y, k, :, half:width] + a_recv[1, k].astype(f32)
    b_out[1] = a_sum[1, 1 - x].astype(bf16)
    begun.append(send(6, b_out.at[1], b_recv.at[1], x_peer))
    begun[4].wait_recv()
    s_send[2] = s_send[1] + s_recv[1]
    begun.append(send(7, s_send.at[2], s_recv.at[2], y_peer))

    begun[5].wait_recv()
    main_o[:, 0:half] = a_sum[0, y] + b_recv[0].astype(f32)
    begun[6].wait_recv()
    main_o[:, half:width] = a_sum[1, x] + b_recv[1].astype(f32)
    begun[7].wait_recv()
    small_o[...] = s_send[2] + s_recv[2]
    for copy in begun:
        copy.wait_send()


def scatter_grads(ga, small2, small3, gb, qb):
    n_dp, depth, width = ga.shape
    half = width // 2
    dma = pltpu.SemaphoreType.DMA
    return pl.pallas_call(
        scatter_kernel,
        name="scatter",
        in_specs=[ANY, VMEM, VMEM, VMEM, VMEM],
        out_specs=[VMEM, VMEM],
        out_shape=[struct((depth, width), f32), struct((16, width), f32)],
        scratch_shapes=[
            pltpu.VMEM((2, 2, depth, width), bf16),
            pltpu.VMEM((2, 2, depth, width), bf16),
            pltpu.VMEM((2, 2, depth, width), f32),
            pltpu.VMEM((2, 2, depth, half), bf16),
            pltpu.VMEM((2, 2, depth, half), bf16),
            pltpu.VMEM((2, 2, depth, half), f32),
            pltpu.VMEM((2, depth, half), bf16),
            pltpu.VMEM((2, depth, half), bf16),
            pltpu.VMEM((3, 16, width), f32),
            pltpu.VMEM((3, 16, width), f32),
            dma((1,)),
            dma((8,)),
            dma((8,)),
        ],
        compiler_params=pltpu.CompilerParams(
            vmem_limit_bytes=32 * 2**20, collective_id=1, has_side_effects=True
        ),
    )(ga.reshape(2, 2, 2, depth, width), small2, small3, gb, qb)


def run_group(patches, counts, kept, cot, vec, qkv_b, fc1_b, wqkv, wproj, fcs, me, own):
    images, patch_count, width = patches.shape
    slot_count = cot.shape[1]
    inner = wproj.shape[1]
    pairs = inner // KEYS
    _, groups, _, unit = fcs.shape
    cap = -(-images * ROWS // BLOCK) * BLOCK
    nmax = cap // BLOCK
    dma = pltpu.SemaphoreType.DMA
    vis, gm, qkv, att, mid = pl.pallas_call(
        functools.partial(attend_kernel, images, pairs),
        name="attend",
        in_specs=[SMEM, VMEM, ANY, ANY, ANY, ANY, VMEM, VMEM],
        out_specs=[ANY] * 5,
        out_shape=[
            struct((cap, width), bf16),
            struct((cap, width), bf16),
            struct((cap, 3 * inner), bf16),
            struct((cap, inner), bf16),
            struct((cap, width), f32),
        ],
        scratch_shapes=[
            pltpu.SMEM((images,), jnp.int32),
            pltpu.VMEM((images, patch_count, width), bf16),
            pltpu.VMEM((images, ROWS, width), bf16),
            pltpu.VMEM((width, 3 * inner), bf16),
            pltpu.VMEM((width, inner), bf16),
            pltpu.VMEM((cap + KEYS, width), bf16),
            pltpu.VMEM((cap + KEYS, width), bf16),
            pltpu.VMEM((cap + KEYS, 3 * inner), bf16),
            pltpu.VMEM((cap + KEYS, inner), bf16),
            pltpu.VMEM((cap, width), f32),
            dma((images,)),
            dma((images,)),
            dma((5, nmax)),
            dma((2,)),
        ],
        **PARAMS,
    )(counts, kept, patches, cot, wqkv, wproj, vec, qkv_b)
    out, gmid, gfc, gb, small2 = pl.pallas_call(
        functools.partial(mlp_kernel, images, groups),
        name="mlp",
        in_specs=[SMEM, SMEM, ANY, ANY, ANY, VMEM, VMEM],
        out_specs=[ANY, ANY, VMEM, VMEM, VMEM],
        out_shape=[
            struct((images, slot_count, width), bf16),
            struct((cap, width), f32),
            struct((width, 2 * unit), bf16),
            struct((8, unit), f32),
            struct((3, 8, width), f32),
        ],
        scratch_shapes=[
            pltpu.SMEM((images,), jnp.int32),
            pltpu.VMEM((cap, width), f32),
            pltpu.VMEM((cap, width), bf16),
            pltpu.VMEM((cap + KEYS, width), bf16),
            pltpu.VMEM((images, slot_count, width), bf16),
            pltpu.VMEM((2, width, unit), f32),
            pltpu.VMEM((groups, 2, width, unit), bf16),
            dma((2, nmax)),
            dma((nmax,)),
            dma((images,)),
            dma((groups,)),
        ],
        **PARAMS,
    )(me, counts, mid, gm, fcs, vec, fc1_b)
    window = -(-own // KEYS) * KEYS
    pg, ga, small3, qb = pl.pallas_call(
        functools.partial(back_kernel, images, pairs),
        name="back",
        in_specs=[SMEM, SMEM, VMEM, ANY, ANY, ANY, ANY, ANY, ANY, VMEM],
        out_specs=[ANY, VMEM, VMEM, VMEM],
        out_shape=[
            struct((patch_count, images, width), f32),
            struct((width, 4 * own), bf16),
            struct((3, 8, width), f32),
            struct((2, 8, own), f32),
        ],
        scratch_shapes=[
            pltpu.SMEM((images,), jnp.int32),
            pltpu.VMEM((3, BLOCK, width), f32),
            pltpu.VMEM((cap + KEYS, 3 * inner), bf16),
            pltpu.VMEM((cap, window), bf16),
            pltpu.VMEM((cap, width), bf16),
            pltpu.VMEM((cap + KEYS, inner), bf16),
            pltpu.VMEM((cap + KEYS, 3 * inner), bf16),
            pltpu.VMEM((width, 3 * window), f32),
            pltpu.VMEM((width, window), f32),
            pltpu.VMEM((2, 8, window), f32),
            pltpu.VMEM((4, patch_count, width), f32),
            pltpu.VMEM((width, 3 * inner), bf16),
            pltpu.VMEM((width, inner), bf16),
            dma((3, nmax)),
            dma((4,)),
            dma((2,)),
            dma((3,)),
        ],
        **PARAMS,
    )(me, counts, kept, gmid, qkv, att, vis, wqkv, wproj, vec)
    return out, pg.transpose(1, 0, 2), (gfc, ga, small2, small3, gb, qb)


def per_device(
    patches,
    counts,
    kept_patches,
    cotangent,
    norm_gains,
    shifts,
    qkv_weight,
    qkv_bias,
    proj_weight,
    fc1_weight,
    fc1_bias,
    fc2_weight,
):
    image_count, patch_count, width = patches.shape
    n_mp = lax.axis_size("mp")
    me = lax.axis_index("mp").astype(jnp.int32).reshape(1)
    own = qkv_weight.shape[2]
    inner = own * n_mp

    n_dp = lax.axis_size("dp")
    depth = width // n_dp
    direct = n_dp == 8 and n_mp == 4 and depth % 16 == 0
    if direct:
        wqkv, wproj, fcs, vec, qkv_b, fc1_b = gather_weights(
            qkv_weight.transpose(1, 0, 2), proj_weight, fc1_weight, fc2_weight.T,
            norm_gains, shifts, qkv_bias, fc1_bias.reshape(1, -1), n_dp, n_mp,
        )
    else:
        vec = lax.all_gather(jnp.concatenate([norm_gains, shifts]), "dp", axis=1, tiled=True)
        vec = jnp.pad(vec.astype(f32), ((0, 2), (0, 0)))
        wqkv = lax.all_gather(lax.all_gather(qkv_weight, "mp", axis=2, tiled=True), "dp", axis=0, tiled=True)
        wqkv = wqkv.reshape(width, 3 * inner)
        qkv_b = lax.all_gather(qkv_bias, "mp", axis=1, tiled=True).astype(f32)
        wproj = lax.all_gather(lax.all_gather(proj_weight.T, "mp", axis=1, tiled=True), "dp", axis=0, tiled=True)
        both = jnp.stack([fc1_weight, fc2_weight.T])
        fcs = lax.all_gather(lax.all_gather(both, "mp", axis=1), "dp", axis=2, tiled=True)
        fc1_b = lax.all_gather(fc1_bias, "mp", axis=0).astype(f32)

    group = max(n for n in range(1, GROUP_MAX + 1) if image_count % n == 0)
    outs, pgs, grads = [], [], []
    for first in range(0, image_count, group):
        part = slice(first, first + group)
        out, pg, grad = run_group(
            patches[part], counts[part], kept_patches[part], cotangent[part],
            vec, qkv_b, fc1_b, wqkv, wproj, fcs, me, own,
        )
        outs.append(out)
        pgs.append(pg)
        grads.append(grad)
    if len(grads) > 1:
        grads = [tuple(sum(item.astype(f32) for item in items) for items in zip(*grads))]
    gfc, ga, small2, small3, gb, qb = grads[0]
    hid = fc1_weight.shape[1]
    gfc = lax.psum_scatter(gfc.astype(bf16), "dp", scatter_dimension=0, tiled=True).astype(f32)
    if direct:
        main, small = scatter_grads(ga.astype(bf16).reshape(n_dp, depth, -1), small2, small3, gb, qb)
    else:
        main = lax.psum_scatter(ga.astype(bf16), "dp", scatter_dimension=0, tiled=True).astype(f32)
        rows = [small3[0], small2[0], small3[2], small3[1], small2[1], small2[2], gb]
        rows += [jnp.pad(qb[n], ((0, 0), (0, width - own))) for n in range(2)]
        small = lax.psum(jnp.stack([jnp.sum(row, axis=0) for row in rows]), "dp")
    mine = lax.dynamic_slice_in_dim(small[:6], lax.axis_index("dp") * depth, depth, 1)
    return (
        outs[0] if len(outs) == 1 else jnp.concatenate(outs, axis=0),
        pgs[0] if len(pgs) == 1 else jnp.concatenate(pgs, axis=0),
        mine[:2],
        mine[2:],
        jnp.stack([main[:, j * own : (j + 1) * own] for j in range(3)]).transpose(1, 0, 2),
        small[7:9, :own],
        main[:, 3 * own : 4 * own].T,
        gfc[:, :hid],
        small[6],
        gfc[:, hid:].T,
    )


def solution(mesh):
    placed = (
        P("dp", None, None),
        P("dp"),
        P("dp", None),
        P("dp", None, None),
        P(None, "dp"),
        P(None, "dp"),
        P("dp", None, "mp"),
        P(None, "mp"),
        P("mp", "dp"),
        P("dp", "mp"),
        P("mp"),
        P("mp", "dp"),
    )
    return jax.shard_map(
        per_device,
        mesh=mesh,
        in_specs=placed,
        out_specs=(
            P("dp", None, None),
            P("dp", None, None),
            P(None, "dp"),
            P(None, "dp"),
            P("dp", None, "mp"),
            P(None, "mp"),
            P("mp", "dp"),
            P("dp", "mp"),
            P("mp"),
            P("mp", "dp"),
        ),
        check_vma=False,
    )
```

```python
import functools

import jax
import jax.numpy as jnp
from jax import lax
from jax.experimental import pallas as pl
from jax.experimental.pallas import tpu as pltpu
from jax.sharding import PartitionSpec as P

HD = 64
KEEP_MAX = 98
ROWS = 112
ROW_CHOICES = (64, 80, 96, 112)
KEYS = 128
BLOCK = 256
PAIRS_AT_ONCE = 6
GROUP_MAX = 24
EPSILON = 1e-06
VMEM_BYTES = 59 * 2**20

f32 = jnp.float32
bf16 = jnp.bfloat16

NN = (((1,), (0,)), ((), ()))
NT = (((1,), (1,)), ((), ()))
TN = (((0,), (0,)), ((), ()))


def dot(left, right, dims=NN):
    return lax.dot_general(left, right, dims, preferred_element_type=f32)


def norm_stats(values):
    row_mean = jnp.mean(values, axis=-1, keepdims=True)
    centred = values - row_mean
    inverse = lax.rsqrt(jnp.mean(centred * centred, axis=-1, keepdims=True) + EPSILON)
    return centred * inverse, inverse


def norm_pull(grad_normed, normed, inverse, gain_row):
    scaled = grad_normed * gain_row
    first_mean = jnp.mean(scaled, axis=-1, keepdims=True)
    second_mean = jnp.mean(scaled * normed, axis=-1, keepdims=True)
    return inverse * (scaled - first_mean - normed * second_mean)


def fold_rows(values):
    rows, width = values.shape
    return jnp.sum(values.reshape(rows // 8, 8, width), axis=0)


def gelu_parts(u):
    bell = jnp.exp(u * u * -0.5)
    t = 1.0 / (1.0 + 0.23164190 * jnp.abs(u))
    poly = 0.5307027145
    for c in (-0.7265760135, 0.7107068705, -0.142248368, 0.127414796):
        poly = poly * t + c
    tail = poly * t * bell
    cdf = jnp.where(u >= 0, 1.0 - tail, tail)
    return u * cdf, cdf + u * bell * 0.3989422804014327


def fill_offsets(counts, offs, images):
    def step(i, total):
        offs[i] = total
        return total + lax.div(counts[i] + 15, 16) * 16

    total = lax.fori_loop(0, images, step, 0)
    return lax.div(total + BLOCK - 1, BLOCK)


def lane_split(values):
    left = lax.broadcasted_iota(jnp.int32, values.shape, 1) < HD
    zero = jnp.zeros_like(values)
    return jnp.concatenate([jnp.where(left, values, zero), jnp.where(left, zero, values)], axis=0)


def head_marks():
    shape = (2 * KEYS, KEYS)
    first = lax.broadcasted_iota(jnp.int32, shape, 0) < KEYS
    left = lax.broadcasted_iota(jnp.int32, shape, 1) < HD
    return jnp.where(first == left, 1.0, 0.0).astype(bf16)


def with_marks(values):
    return jnp.concatenate([lane_split(values), head_marks()], axis=1)


def row_block(b):
    return pl.ds(pl.multiple_of(b * BLOCK, BLOCK), BLOCK)


def by_rows(count, body):
    low = 0
    for rows in ROW_CHOICES:
        @pl.when((count > low) & (count <= rows))
        def _(rows=rows):
            body(rows)

        low = rows


def attend_kernel(
    images, pairs, counts, kept, patches, cot, wqkv, wproj, vec, bias,
    vis_o, gm_o, qkv_o, att_o, mid_o,
    offs, pbuf, cbuf, wqkv_v, wproj_v, vis, gm, qkv, att, mid,
    in_sem, cot_sem, blk_sem, w_sem,
):
    width = vis.shape[1]
    inner = att.shape[1]
    nblk = fill_offsets(counts, offs, images)

    def patch_copy(i):
        return pltpu.make_async_copy(patches.at[i], pbuf.at[i], in_sem.at[i])

    def cot_copy(i):
        return pltpu.make_async_copy(cot.at[i, pl.ds(0, ROWS)], cbuf.at[i], cot_sem.at[i])

    def start_in(i, carry):
        patch_copy(i).start()
        cot_copy(i).start()
        return carry

    lax.fori_loop(0, images, start_in, 0)
    load_qkv = pltpu.make_async_copy(wqkv, wqkv_v, w_sem.at[0])
    load_proj = pltpu.make_async_copy(wproj, wproj_v, w_sem.at[1])
    load_qkv.start()
    load_proj.start()

    def clear(b, carry):
        rows = row_block(b)
        vis[rows, :] = jnp.zeros((BLOCK, width), bf16)
        gm[rows, :] = jnp.zeros((BLOCK, width), bf16)
        att[rows, :] = jnp.zeros((BLOCK, inner), bf16)
        return carry

    lax.fori_loop(0, nblk, clear, 0)
    after = pl.ds(pl.multiple_of(nblk * BLOCK, BLOCK), KEYS)
    qkv[after, :] = jnp.zeros((KEYS, qkv.shape[1]), bf16)

    def gather(i, carry):
        patch_copy(i).wait()
        cot_copy(i).wait()
        off = pl.multiple_of(offs[i], 16)
        kept_row = kept[pl.ds(i, 1), :]
        patch_ids = lax.broadcasted_iota(jnp.int32, (pbuf.shape[1], KEYS), 0)
        onehot = jnp.where(patch_ids == kept_row, 1.0, 0.0).astype(bf16)
        vis[pl.ds(off, KEYS), :] = dot(onehot, pbuf[i], TN).astype(bf16)
        live = lax.broadcasted_iota(jnp.int32, (ROWS, width), 0) < counts[i]
        gm[pl.ds(off, ROWS), :] = jnp.where(live, cbuf[i], jnp.zeros((ROWS, width), bf16))
        return carry

    lax.fori_loop(0, images, gather, 0)

    def out_copies(b, which=(0, 1, 2, 3, 4)):
        rows = row_block(b)
        pairs_of = ((vis, vis_o), (gm, gm_o), (qkv, qkv_o), (att, att_o), (mid, mid_o))
        return [
            pltpu.make_async_copy(pairs_of[n][0].at[rows], pairs_of[n][1].at[rows], blk_sem.at[n, b])
            for n in which
        ]

    def project(b, carry):
        rows = row_block(b)
        normed, _ = norm_stats(vis[rows, :].astype(f32))
        source = (normed * vec[0:1, :] + vec[2:3, :]).astype(bf16)
        for j in range(3):
            cols = slice(j * inner, (j + 1) * inner)
            part = dot(source, wqkv_v[:, cols])
            if j == 0:
                part = (part + bias[0:1, :]) * (HD**-0.5)
            if j == 2:
                part = part + bias[1:2, :]
            qkv[rows, cols] = part.astype(bf16)
        for copy in out_copies(b, (0, 1, 2)):
            copy.start()
        return carry

    load_qkv.wait()
    lax.fori_loop(0, nblk, project, 0)

    def attend(i, carry):
        off = pl.multiple_of(offs[i], 16)
        count = counts[i]

        def body(rows):
            key_live = lax.broadcasted_iota(jnp.int32, (rows, KEYS), 1) < count
            held = []
            for p in range(pairs):
                c = p * KEYS
                q2 = qkv[pl.ds(off, rows), c : c + KEYS]
                k2 = qkv[pl.ds(off, KEYS), inner + c : inner + c + KEYS]
                v2 = qkv[pl.ds(off, KEYS), 2 * inner + c : 2 * inner + c + KEYS]
                held.append((c, v2, dot(q2, lane_split(k2), NT)))
            ready = []
            for c, v2, scores in held:
                halves = []
                for h in range(2):
                    s = jnp.where(key_live, scores[:, h * KEYS : (h + 1) * KEYS], -1e30)
                    halves.append(jnp.exp(s - jnp.max(s, axis=-1, keepdims=True)).astype(bf16))
                ready.append((c, v2, jnp.concatenate(halves, axis=1)))
            done = [(c, dot(ex, with_marks(v2))) for c, v2, ex in ready]
            for c, both in done:
                att[pl.ds(off, rows), c : c + KEYS] = (both[:, :KEYS] / both[:, KEYS:]).astype(bf16)

        by_rows(count, body)
        return carry

    lax.fori_loop(0, images, attend, 0)
    load_proj.wait()

    def finish(b, carry):
        rows = row_block(b)
        attention = dot(att[rows, :], wproj_v[...], NT) + vec[3:4, :]
        mid[rows, :] = vis[rows, :].astype(f32) + attention
        for copy in out_copies(b, (3, 4)):
            copy.start()
        return carry

    lax.fori_loop(0, nblk, finish, 0)

    def drain(b, carry):
        for copy in out_copies(b):
            copy.wait()
        return carry

    lax.fori_loop(0, nblk, drain, 0)


def mlp_kernel(
    images, groups, me_ref, counts, mid_h, gm_h, fc1, fc2, vec, bias,
    out_o, gmid_o, gfc_o, gb_o, small_o,
    offs, mid, gm, out, stage, acc, w1, w2, in_sem, gmid_sem, out_sem, w_sem,
):
    width = mid.shape[1]
    me = me_ref[0]
    nblk = fill_offsets(counts, offs, images)

    def in_copies(b):
        rows = row_block(b)
        return (
            pltpu.make_async_copy(mid_h.at[rows], mid.at[rows], in_sem.at[0, b]),
            pltpu.make_async_copy(gm_h.at[rows], gm.at[rows], in_sem.at[1, b]),
        )

    def start_in(b, carry):
        for copy in in_copies(b):
            copy.start()
        return carry

    lax.fori_loop(0, nblk, start_in, 0)

    def loads(s):
        g = lax.rem(me + s, groups)
        return [
            pltpu.make_async_copy(fc1.at[g], w1.at[s], w_sem.at[0, s]),
            pltpu.make_async_copy(fc2.at[:, g], w2.at[s], w_sem.at[1, s]),
        ]

    for s in range(groups):
        for copy in loads(s):
            copy.start()

    def flat(ref, s):
        value = ref[s]
        return value.reshape(value.shape[0] * value.shape[1], value.shape[2])

    acc[...] = jnp.zeros_like(acc)
    gb_o[...] = jnp.zeros_like(gb_o)
    small_o[...] = jnp.zeros_like(small_o)

    def gmid_copy(b):
        rows = row_block(b)
        return pltpu.make_async_copy(mid.at[rows], gmid_o.at[rows], gmid_sem.at[b])

    def block(b, carry):
        rows = row_block(b)
        for copy in in_copies(b):
            copy.wait()
        normed, inverse = norm_stats(mid[rows, :])
        source = (normed * vec[1:2, :] + vec[4:5, :]).astype(bf16)
        gmb = gm[rows, :]
        sums = [None, None]
        opened, kept_back = {}, {}

        def open_group(s):
            g = lax.rem(me + s, groups)
            pre = dot(source, flat(w1, s)) + bias[pl.ds(g, 1), :]
            opened[s] = (pre, dot(gmb, flat(w2, s)))

        def close_group(s):
            pre, grad_act = opened.pop(s)
            act, slope = gelu_parts(pre)
            act = act.astype(bf16)
            gp = (grad_act * slope).astype(bf16)
            parts = (dot(act, flat(w2, s), NT), dot(gp, flat(w1, s), NT))
            for n in range(2):
                sums[n] = parts[n] if sums[n] is None else sums[n] + parts[n]
            if s == 0:
                kept_back["own"] = (act, gp)

        open_group(0)
        for s in range(groups):
            if s + 1 < groups:
                open_group(s + 1)
            close_group(s)
        mlp, gnm = sums
        act, gp = kept_back["own"]
        acc[0] += dot(source, gp, TN)
        acc[1] += dot(gmb, act, TN)
        gb_o[...] += fold_rows(gp.astype(f32))
        out[rows, :] = (mid[rows, :] + mlp + vec[5:6, :]).astype(bf16)
        grad_mid = gmb.astype(f32) + norm_pull(gnm, normed, inverse, vec[1:2, :])
        small_o[0] += fold_rows(gnm * normed)
        small_o[1] += fold_rows(gnm)
        small_o[2] += fold_rows(gmb.astype(f32))
        mid[rows, :] = grad_mid
        gmid_copy(b).start()
        return carry

    for s in range(groups):
        for copy in loads(s):
            copy.wait()
    lax.fori_loop(0, nblk, block, 0)
    for n in range(2):
        gfc_o[:, n * acc.shape[2] : (n + 1) * acc.shape[2]] = acc[n].astype(bf16)

    def out_copy(i):
        return pltpu.make_async_copy(stage.at[i], out_o.at[i], out_sem.at[i])

    def unpack(i, carry):
        off = pl.multiple_of(offs[i], 16)
        slots = stage.shape[1]
        live = lax.broadcasted_iota(jnp.int32, (ROWS, width), 0) < counts[i]
        stage[i, pl.ds(0, ROWS), :] = jnp.where(live, out[pl.ds(off, ROWS), :], jnp.zeros((ROWS, width), bf16))
        if slots > ROWS:
            stage[i, pl.ds(ROWS, slots - ROWS), :] = jnp.zeros((slots - ROWS, width), bf16)
        out_copy(i).start()
        return carry

    lax.fori_loop(0, images, unpack, 0)

    def drain(i, carry):
        out_copy(i).wait()
        return carry

    lax.fori_loop(0, images, drain, 0)

    def drain_gmid(b, carry):
        gmid_copy(b).wait()
        return carry

    lax.fori_loop(0, nblk, drain_gmid, 0)


def back_kernel(
    images, pairs, me_ref, counts, kept, gmid_h, qkv_h, att_h, vis_h, wqkv, wproj, vec,
    pg_o, ga_o, small_o, qb_o,
    offs, gmid, qkv, att, vis, gat, dqkv, accq, accp, qsum, stage, wqkv_v, wproj_v,
    in_sem, pg_sem, w_sem, gmid_sem,
):
    width = vis.shape[1]
    inner = gat.shape[1]
    me = me_ref[0]
    own = qb_o.shape[2]
    window = accp.shape[1]
    start = pl.multiple_of(lax.div(me * own, KEYS) * KEYS, KEYS)
    nblk = fill_offsets(counts, offs, images)

    def in_copies(b, which=(0, 1, 2)):
        rows = row_block(b)
        pairs_of = (
            (att_h.at[rows, pl.ds(start, window)], att),
            (qkv_h.at[rows], qkv),
            (vis_h.at[rows], vis),
        )
        return [
            pltpu.make_async_copy(pairs_of[n][0], pairs_of[n][1].at[rows], in_sem.at[n, b])
            for n in which
        ]

    load_proj = pltpu.make_async_copy(wproj, wproj_v, w_sem.at[0])
    load_qkv = pltpu.make_async_copy(wqkv, wqkv_v, w_sem.at[1])
    load_proj.start()
    depth = gmid.shape[0]

    def gmid_copy(b):
        slot = lax.rem(b, depth)
        return pltpu.make_async_copy(gmid_h.at[row_block(b)], gmid.at[slot], gmid_sem.at[slot])

    def gmid_begin():
        for b in range(depth - 1):
            @pl.when(b < nblk)
            def _(b=b):
                gmid_copy(b).start()

    def gmid_block(b):
        gmid_copy(b).wait()

        @pl.when(b + depth - 1 < nblk)
        def _():
            gmid_copy(b + depth - 1).start()

        return gmid[lax.rem(b, depth)]

    gmid_begin()

    def start_first(b, carry):
        for copy in in_copies(b, (0,)):
            copy.start()
        return carry

    def start_rest(b, carry):
        for copy in in_copies(b, (1, 2)):
            copy.start()
        return carry

    lax.fori_loop(0, nblk, start_first, 0)
    lax.fori_loop(0, nblk, start_rest, 0)
    load_qkv.start()
    accq[...] = jnp.zeros_like(accq)
    accp[...] = jnp.zeros_like(accp)
    small_o[...] = jnp.zeros_like(small_o)
    qsum[...] = jnp.zeros_like(qsum)

    def first(b, carry):
        rows = row_block(b)
        for copy in in_copies(b, (0,)):
            copy.wait()
        ga = gmid_block(b).astype(bf16)
        small_o[1] += fold_rows(ga.astype(f32))
        gat[rows, :] = dot(ga, wproj_v[...]).astype(bf16)
        accp[...] += dot(ga, att[rows, :], TN)
        dqkv[rows, :] = jnp.zeros((BLOCK, dqkv.shape[1]), bf16)
        return carry

    load_proj.wait()
    lax.fori_loop(0, nblk, first, 0)
    after = pl.ds(pl.multiple_of(nblk * BLOCK, BLOCK), KEYS)
    qkv[after, :] = jnp.zeros((KEYS, qkv.shape[1]), bf16)
    gat[after, :] = jnp.zeros((KEYS, inner), bf16)

    def wait_rest(b, carry):
        for copy in in_copies(b, (1, 2)):
            copy.wait()
        return carry

    lax.fori_loop(0, nblk, wait_rest, 0)

    gmid_begin()

    def attend(i, carry):
        off = pl.multiple_of(offs[i], 16)
        count = counts[i]
        left = lax.broadcasted_iota(jnp.int32, (KEYS, KEYS), 1) < HD
        row_live = lax.broadcasted_iota(jnp.int32, (KEYS, KEYS), 0) < count
        square = (KEYS, KEYS)
        eye = jnp.where(
            lax.broadcasted_iota(jnp.int32, square, 0) == lax.broadcasted_iota(jnp.int32, square, 1), 1.0, 0.0
        ).astype(bf16)

        def body(rows):
            key_live = lax.broadcasted_iota(jnp.int32, (rows, 2 * KEYS), 0) < count
            here = pl.ds(off, rows)
            wide = pl.ds(off, KEYS)
            for first in range(0, pairs, PAIRS_AT_ONCE):
                held = []
                for p in range(first, min(first + PAIRS_AT_ONCE, pairs)):
                    c = p * KEYS
                    qs = lane_split(qkv[wide, c : c + KEYS])
                    k2 = qkv[here, inner + c : inner + c + KEYS]
                    v2 = qkv[here, 2 * inner + c : 2 * inner + c + KEYS]
                    do2 = gat[wide, c : c + KEYS]
                    ds = lane_split(jnp.where(row_live, do2, jnp.zeros_like(do2)))
                    held.append((c, qs, k2, ds, dot(k2, qs, NT), dot(v2, ds, NT)))
                ready = []
                for c, qs, k2, ds, st, slope in held:
                    st = jnp.where(key_live, st, -1e30)
                    e = jnp.exp(st - jnp.max(st, axis=0, keepdims=True))
                    pr = e * (1.0 / jnp.sum(e, axis=0, keepdims=True))
                    delta = jnp.sum(pr * slope, axis=0, keepdims=True)
                    gs = (pr * (slope - delta)).astype(bf16)
                    ready.append((c, qs, k2, ds, pr.astype(bf16), gs))
                done = []
                for c, qs, k2, ds, pr, gs in ready:
                    dq_a = dot(gs[:, :KEYS], k2, TN)
                    dq_b = dot(gs[:, KEYS:], k2, TN)
                    dq = jnp.where(left, dq_a, dq_b)[:rows] * (HD**-0.5)
                    done.append((c, dq, dot(gs, qs), dot(pr, ds)))
                for c, dq, dk, dv in done:
                    dqkv[here, c : c + KEYS] = dq.astype(bf16)
                    dqkv[here, inner + c : inner + c + KEYS] = dk.astype(bf16)
                    dqkv[here, 2 * inner + c : 2 * inner + c + KEYS] = dv.astype(bf16)

        by_rows(count, body)
        return carry

    lax.fori_loop(0, images, attend, 0)

    def second(b, carry):
        rows = row_block(b)
        normed, inverse = norm_stats(vis[rows, :].astype(f32))
        source = (normed * vec[0:1, :] + vec[2:3, :]).astype(bf16)
        gni = dot(dqkv[rows, :], wqkv_v[...], NT)
        small_o[0] += fold_rows(gni * normed)
        small_o[2] += fold_rows(gni)
        mine = jnp.concatenate(
            [dqkv[rows, pl.ds(pl.multiple_of(j * inner + start, KEYS), window)] for j in range(3)], axis=1
        )
        accq[...] += dot(source, mine, TN)
        qsum[0] += fold_rows(mine[:, :window].astype(f32))
        qsum[1] += fold_rows(mine[:, 2 * window :].astype(f32))
        grad = gmid_block(b) + norm_pull(gni, normed, inverse, vec[0:1, :])
        gat[rows, :] = grad.astype(bf16)
        return carry

    load_qkv.wait()
    lax.fori_loop(0, nblk, second, 0)

    slots = stage.shape[0]

    def pg_copy(i):
        slot = lax.rem(i, slots)
        return pltpu.make_async_copy(stage.at[slot], pg_o.at[:, i], pg_sem.at[slot])

    def scatter(i, carry):
        @pl.when(i >= slots)
        def _():
            pg_copy(i - slots).wait()

        off = pl.multiple_of(offs[i], 16)
        kept_row = kept[pl.ds(i, 1), :]
        shape = (stage.shape[1], KEYS)
        hit = (lax.broadcasted_iota(jnp.int32, shape, 0) == kept_row) & (
            lax.broadcasted_iota(jnp.int32, shape, 1) < counts[i]
        )
        onehot = jnp.where(hit, 1.0, 0.0).astype(bf16)
        stage[lax.rem(i, slots)] = dot(onehot, gat[pl.ds(off, KEYS), :])
        pg_copy(i).start()
        return carry

    lax.fori_loop(0, images, scatter, 0)

    def drain(i, carry):
        pg_copy(i).wait()
        return carry

    lax.fori_loop(max(0, images - slots), images, drain, 0)

    def emit(shift):
        ga_o[:, 3 * own : 4 * own] = accp[:, shift : shift + own].astype(bf16)
        for j in range(3):
            ga_o[:, j * own : (j + 1) * own] = accq[:, j * window + shift : j * window + shift + own].astype(bf16)
        for n in range(2):
            qb_o[n] = qsum[n, :, shift : shift + own]

    shift = me * own - start

    @pl.when(shift == 0)
    def _():
        emit(0)

    @pl.when(shift != 0)
    def _():
        emit(window - own)


SMEM = pl.BlockSpec(memory_space=pltpu.SMEM)
VMEM = pl.BlockSpec(memory_space=pltpu.VMEM)
ANY = pl.BlockSpec(memory_space=pltpu.HBM)
PARAMS = dict(compiler_params=pltpu.CompilerParams(vmem_limit_bytes=VMEM_BYTES))


def struct(shape, dtype):
    return jax.ShapeDtypeStruct(shape, dtype)


MESH = pl.DeviceIdType.MESH
SMALL_ROWS = 16


def greet(peers):
    barrier = pltpu.get_barrier_semaphore()
    for peer in peers:
        pl.semaphore_signal(barrier, inc=1, device_id=peer, device_id_type=MESH)
    pl.semaphore_wait(barrier, len(peers))


def gather_kernel(
    n_mp, qkv_w, proj_w, fc1_w, fc2_w, gains, shifts, qkv_b, fc1_b, patches,
    wqkv_o, wproj_o, fc1_o, fc2_o, patches_o, vec_o, qb_o, fb_o,
    held, fc1, fc2, wqkv, wproj, notes, raw, plain, spread_out,
    own_sem, out_sem, patch_sem, send_sem, recv_sem,
):
    g = lax.axis_index("mp")
    d = lax.axis_index("dp")
    depth, width = fc1_w.shape
    part = qkv_w.shape[2]
    x_peer, y_peer, twin = d ^ 2, d ^ 4, d ^ 1
    upper = g // 2
    inner = (g == 1) | (g == 2)
    mate, facing = g ^ 1, 3 - g
    across = [g, mate, 2 - upper, 3 - 3 * upper]
    peers = [(d, g ^ s) for s in range(1, n_mp)] + [(x_peer, g), (y_peer, g), (twin, g)]
    barrier = pltpu.get_barrier_semaphore()
    for peer in peers:
        pl.semaphore_signal(barrier, inc=1, device_id=peer, device_id_type=MESH)
    own1 = pltpu.make_async_copy(fc1_w, fc1.at[g, d], own_sem.at[0])
    own2 = pltpu.make_async_copy(fc2_w, fc2.at[g], own_sem.at[1])
    own1.start()
    own2.start()
    for j in range(3):
        held[g, d, 0:depth, j * part : (j + 1) * part] = qkv_w[j]
    held[g, d, 0:depth, 3 * part : 4 * part] = proj_w[...].astype(f32).T.astype(bf16)
    notes[...] = jnp.zeros_like(notes)
    notes[0:2, 0:depth] = gains[...].astype(f32)
    notes[2:6, 0:depth] = shifts[...].astype(f32)
    notes[6:8, 0:part] = qkv_b[...].astype(f32)
    notes[8:9, :] = fc1_b[...].astype(f32)
    held[g, d, depth : depth + SMALL_ROWS, :] = notes[...].astype(bf16)
    pl.semaphore_wait(barrier, len(peers))

    half = width // 2
    halves = (slice(0, half), slice(half, width))
    firsts = (x_peer, y_peer)
    others = (y_peer, x_peer)
    number = {}

    def place(u, gg, dd, cols=None):
        if u == 2:
            return fc2.at[gg]
        ref = held if u == 0 else fc1
        return ref.at[gg, dd] if cols is None else ref.at[gg, dd, :, cols]

    def send(key, ref, peer, relay=False):
        k = number.setdefault(key, len(number))
        out = number.setdefault(("relay",) + key, len(number)) if relay else k
        return pltpu.make_async_remote_copy(
            src_ref=ref, dst_ref=ref, send_sem=send_sem.at[out], recv_sem=recv_sem.at[k],
            device_id=peer, device_id_type=MESH,
        )

    begun, crossed = [], []

    def begin_inner(key, ref, peer, relay=False):
        @pl.when(inner)
        def _():
            send(key, ref, peer, relay).start()

        crossed.append((key, ref, peer, relay))

    def begin(key, ref, peer):
        copy = send(key, ref, peer)
        copy.start()
        begun.append(copy)

    def arrive(key, ref, peer):
        send(key, ref, peer).wait_recv()

    def cross(u):
        begin(("z", u, 1), place(u, g, d), (d, mate))
        begin_inner(("z", u, 2), place(u, g, d), (d, facing))

    def land(u, s):
        arrive(("z", u, s), place(u, across[s], d), (d, across[s]))
        if s == 1:
            begin_inner(("z", u, 3), place(u, mate, d), (d, facing))
        else:
            begin_inner(("z", u, s), place(u, across[s], d), (d, mate), True)

    def stage_a(u, s):
        gg = across[s]
        if s:
            land(u, s)
        for h in range(2):
            begin(("p", u, s, h), place(u, gg, d, halves[h]), (firsts[h], g))
        begin(("c", u, s, 0), place(u, gg, d), (twin, g))

    def stage_b(u, s):
        gg = across[s]
        for h in range(2):
            arrive(("p", u, s, h), place(u, gg, firsts[h], halves[h]), (firsts[h], g))
            begin(("q", u, s, h, 0), place(u, gg, d, halves[h]), (others[h], g))
            begin(("q", u, s, h, 1), place(u, gg, firsts[h], halves[h]), (others[h], g))

    def stage_c(u, s):
        gg = across[s]
        for h in range(2):
            arrive(("q", u, s, h, 0), place(u, gg, others[h], halves[h]), (others[h], g))
            arrive(("q", u, s, h, 1), place(u, gg, d ^ 6, halves[h]), (others[h], g))
        for n, dd in enumerate((x_peer, y_peer, d ^ 6)):
            begin(("c", u, s, n + 1), place(u, gg, dd), (twin, g))

    def stage_d(u, s):
        gg = across[s]
        for n, dd in enumerate((d, x_peer, y_peer, d ^ 6)):
            arrive(("c", u, s, n), place(u, gg, dd ^ 1), (twin, g))

    outs = []

    def write(src, dst):
        copy = pltpu.make_async_copy(src, dst, out_sem.at[len(outs)])
        copy.start()
        outs.append(copy)

    def settle():
        def spread(dd, carry):
            rows = pl.ds(pl.multiple_of(dd * depth, 16), depth)
            for gg in range(n_mp):
                for j in range(3):
                    c = (j * n_mp + gg) * part
                    wqkv[rows, c : c + part] = held[gg, dd, 0:depth, j * part : (j + 1) * part]
                wproj[rows, gg * part : (gg + 1) * part] = held[gg, dd, 0:depth, 3 * part : 4 * part]
            return carry

        lax.fori_loop(0, held.shape[1], spread, 0)
        write(wqkv, wqkv_o)
        write(wproj, wproj_o)
        vec_o[...] = jnp.zeros_like(vec_o)
        qb_o[...] = jnp.zeros_like(qb_o)
        fb_o[...] = jnp.zeros_like(fb_o)
        for dd in range(held.shape[1]):
            piece = held[0, dd, depth : depth + SMALL_ROWS, :].astype(f32)
            vec_o[0:6, dd * depth : (dd + 1) * depth] = piece[0:6, 0:depth]
        for gg in range(n_mp):
            piece = held[gg, 0, depth : depth + SMALL_ROWS, :].astype(f32)
            qb_o[0:2, gg * part : (gg + 1) * part] = piece[6:8, 0:part]
            fb_o[gg : gg + 1, :] = piece[8:9, :]

    chunk = raw.shape[2]
    patch_count = raw.shape[1]

    def raw_copy(k):
        return pltpu.make_async_copy(patches.at[:, pl.ds(k * chunk, chunk)], raw.at[k], patch_sem.at[0, k])

    def patch_copy(k):
        part_of = pl.ds(k * chunk, chunk)
        return pltpu.make_async_copy(spread_out.at[part_of], patches_o.at[part_of], patch_sem.at[1, k])

    for k in range(raw.shape[0]):
        raw_copy(k).start()

    def relayout(k):
        if k >= raw.shape[0]:
            return
        raw_copy(k).wait()
        step = 28

        def widen(n, carry):
            rows = raw[k, pl.ds(n * step, step)].astype(f32)
            flat_rows = pl.ds(pl.multiple_of(n * step * chunk, 8), step * chunk)
            for t in range(width // KEYS):
                plain[t, flat_rows, :] = rows[:, :, t * KEYS : (t + 1) * KEYS].reshape(step * chunk, KEYS)
            return carry

        lax.fori_loop(0, patch_count // step, widen, 0)
        for i in range(chunk):
            for t in range(width // KEYS):
                spread_out[k * chunk + i, :, t * KEYS : (t + 1) * KEYS] = plain[
                    t, pl.ds(i, patch_count, stride=chunk), :
                ].astype(bf16)
        patch_copy(k).start()

    def write_patches():
        for k in range(raw.shape[0]):
            patch_copy(k).wait()

    cross(0)
    stage_a(0, 0)
    own1.wait()
    own2.wait()
    cross(1)
    cross(2)
    order = [(0, 0), (1, 0)] + [(0, s) for s in range(1, n_mp)] + [(1, s) for s in range(1, n_mp)]
    count = len(order)
    last = order.index((0, n_mp - 1))
    for k in range(1, count + 2):
        if k < count:
            stage_a(*order[k])
        if k - 1 < count:
            stage_b(*order[k - 1])
        if 0 <= k - 2 < count:
            stage_c(*order[k - 2])
        if k in (1, 2, 3):
            relayout(k - 1)
        if k >= count - 2 and k - count + 3 < n_mp:
            land(2, k - count + 3)
    for s in range(n_mp):
        stage_d(0, s)
    settle()
    for s in range(n_mp):
        stage_d(1, s)
        write(fc1.at[across[s]], fc1_o.at[across[s]])
    write(fc2, fc2_o)
    write_patches()
    for copy in begun:
        copy.wait_send()

    @pl.when(inner)
    def _():
        for key, ref, peer, relay in crossed:
            send(key, ref, peer, relay).wait_send()

    for copy in outs:
        copy.wait()


def gather_weights(qkv_w, proj_w, fc1_w, fc2_w, gains, shifts, qkv_b, fc1_b, patches, n_dp, n_mp):
    depth, width = fc1_w.shape
    part = qkv_w.shape[2]
    images, patch_count, _ = patches.shape
    transfers = 5 * (n_mp - 1) + 2 * n_mp * 10
    dma = pltpu.SemaphoreType.DMA
    outs = pl.pallas_call(
        functools.partial(gather_kernel, n_mp),
        name="gather",
        in_specs=[VMEM, VMEM, ANY, ANY, VMEM, VMEM, VMEM, VMEM, ANY],
        out_specs=[ANY, ANY, ANY, ANY, ANY, VMEM, VMEM, VMEM],
        out_shape=[
            struct((width, 3 * n_mp * part), bf16),
            struct((width, n_mp * part), bf16),
            struct((n_mp, n_dp, depth, width), bf16),
            struct((n_mp, depth, width), bf16),
            struct((images, patch_count, width), bf16),
            struct((8, width), f32),
            struct((8, n_mp * part), f32),
            struct((8, width), f32),
        ],
        scratch_shapes=[
            pltpu.VMEM((n_mp, n_dp, depth + SMALL_ROWS, width), bf16),
            pltpu.VMEM((n_mp, n_dp, depth, width), bf16),
            pltpu.VMEM((n_mp, depth, width), bf16),
            pltpu.VMEM((width, 3 * n_mp * part), bf16),
            pltpu.VMEM((width, n_mp * part), bf16),
            pltpu.VMEM((SMALL_ROWS, width), f32),
            pltpu.VMEM((images // 8, patch_count, 8, width), bf16),
            pltpu.VMEM((width // KEYS, patch_count * 8, KEYS), f32),
            pltpu.VMEM((images, patch_count, width), bf16),
            dma((2,)),
            dma((n_mp + 3,)),
            dma((2, images // 8)),
            dma((transfers,)),
            dma((transfers,)),
        ],
        compiler_params=pltpu.CompilerParams(
            vmem_limit_bytes=VMEM_BYTES, collective_id=0, has_side_effects=True
        ),
    )(qkv_w, proj_w, fc1_w, fc2_w, gains, shifts, qkv_b, fc1_b, patches.transpose(1, 0, 2))
    wqkv, wproj, fc1, fc2, patches, vec, qb, fb = outs
    fc2 = lax.all_gather(fc2, "dp")
    return wqkv, wproj, fc1, fc2, patches, vec, qb, fb


def scatter_kernel(
    ga, small2, small3, gb, qb, main_o, small_o,
    first, c_recv, c_sum, a_out, a_recv, a_sum, b_out, b_recv, s_send, s_recv, own_sem, send_sem, recv_sem,
):
    g = lax.axis_index("mp")
    d = lax.axis_index("dp")
    y, x, c = d // 4, (d // 2) % 2, d % 2
    x_peer, y_peer, twin = d ^ 2, d ^ 4, d ^ 1
    depth, width = main_o.shape
    half = width // 2
    greet([(x_peer, g), (y_peer, g), (twin, g)])

    def send(k, src, dst, peer):
        copy = pltpu.make_async_remote_copy(
            src_ref=src, dst_ref=dst, send_sem=send_sem.at[k], recv_sem=recv_sem.at[k],
            device_id=(peer, g), device_id_type=MESH,
        )
        copy.start()
        return copy

    begun = [send(0, ga.at[:, :, 1 - c], c_recv, twin)]
    own = pltpu.make_async_copy(ga.at[:, :, c], first, own_sem.at[0])
    own.start()
    total = jnp.concatenate(
        [
            jnp.sum(v, axis=0, keepdims=True)
            for v in (small3[0], small2[0], small3[2], small3[1], small2[1], small2[2], gb[...])
        ],
        axis=0,
    )
    s_send[0, 0:7, :] = total
    s_send[0, 7:9, :] = jnp.zeros((2, width), f32)
    s_send[0, 9:16, :] = jnp.zeros((7, width), f32)
    s_send[0, 7:8, 0 : qb.shape[2]] = jnp.sum(qb[0], axis=0, keepdims=True)
    s_send[0, 8:9, 0 : qb.shape[2]] = jnp.sum(qb[1], axis=0, keepdims=True)
    begun.append(send(1, s_send.at[0], s_recv.at[0], twin))

    own.wait()
    begun[0].wait_recv()
    c_sum[...] = first[...].astype(f32) + c_recv[...].astype(f32)
    for k in range(2):
        a_out[0, k] = c_sum[k, 1 - x, :, 0:half].astype(bf16)
        a_out[1, k] = c_sum[1 - y, k, :, half:width].astype(bf16)
    begun.append(send(2, a_out.at[0], a_recv.at[0], x_peer))
    begun.append(send(3, a_out.at[1], a_recv.at[1], y_peer))
    begun[1].wait_recv()
    s_send[1] = s_send[0] + s_recv[0]
    begun.append(send(4, s_send.at[1], s_recv.at[1], x_peer))

    begun[2].wait_recv()
    for k in range(2):
        a_sum[0, k] = c_sum[k, x, :, 0:half] + a_recv[0, k].astype(f32)
    b_out[0] = a_sum[0, 1 - y].astype(bf16)
    begun.append(send(5, b_out.at[0], b_recv.at[0], y_peer))
    begun[3].wait_recv()
    for k in range(2):
        a_sum[1, k] = c_sum[y, k, :, half:width] + a_recv[1, k].astype(f32)
    b_out[1] = a_sum[1, 1 - x].astype(bf16)
    begun.append(send(6, b_out.at[1], b_recv.at[1], x_peer))
    begun[4].wait_recv()
    s_send[2] = s_send[1] + s_recv[1]
    begun.append(send(7, s_send.at[2], s_recv.at[2], y_peer))

    begun[5].wait_recv()
    main_o[:, 0:half] = a_sum[0, y] + b_recv[0].astype(f32)
    begun[6].wait_recv()
    main_o[:, half:width] = a_sum[1, x] + b_recv[1].astype(f32)
    begun[7].wait_recv()
    small_o[...] = s_send[2] + s_recv[2]
    for copy in begun:
        copy.wait_send()


def finish_kernel(n_dp, d_ref, main, small, gfc, qkv_o, proj_o, fc1_o, fc2_o, gain_o, shift_o, qb_o, fb_o):
    depth = main.shape[0]
    part = proj_o.shape[0]
    hid = fc1_o.shape[1]
    for j in range(3):
        qkv_o[j] = main[:, j * part : (j + 1) * part]
    proj_o[...] = main[:, 3 * part : 4 * part].T
    fc1_o[...] = gfc[:, :hid].astype(f32)
    fc2_o[...] = gfc[:, hid:].astype(f32)
    qb_o[...] = small[7:9, 0:part]
    fb_o[...] = small[6:7, :]
    for n in range(n_dp):
        @pl.when(d_ref[0] == n)
        def _(n=n):
            gain_o[...] = small[0:2, n * depth : (n + 1) * depth]
            shift_o[...] = small[2:6, n * depth : (n + 1) * depth]


def finish(d, main, small, gfc, n_dp):
    depth, width = main.shape
    part, hid = width // 4, gfc.shape[1] // 2
    shapes = [(3, depth, part), (part, depth), (depth, hid), (depth, hid), (2, depth), (4, depth), (2, part), (1, hid)]
    return pl.pallas_call(
        functools.partial(finish_kernel, n_dp),
        name="finish",
        in_specs=[SMEM, VMEM, VMEM, VMEM],
        out_specs=[VMEM] * len(shapes),
        out_shape=[struct(shape, f32) for shape in shapes],
    )(d, main, small, gfc)


def scatter_grads(ga, small2, small3, gb, qb):
    n_dp, depth, width = ga.shape
    half = width // 2
    dma = pltpu.SemaphoreType.DMA
    return pl.pallas_call(
        scatter_kernel,
        name="scatter",
        in_specs=[ANY, VMEM, VMEM, VMEM, VMEM],
        out_specs=[VMEM, VMEM],
        out_shape=[struct((depth, width), f32), struct((16, width), f32)],
        scratch_shapes=[
            pltpu.VMEM((2, 2, depth, width), bf16),
            pltpu.VMEM((2, 2, depth, width), bf16),
            pltpu.VMEM((2, 2, depth, width), f32),
            pltpu.VMEM((2, 2, depth, half), bf16),
            pltpu.VMEM((2, 2, depth, half), bf16),
            pltpu.VMEM((2, 2, depth, half), f32),
            pltpu.VMEM((2, depth, half), bf16),
            pltpu.VMEM((2, depth, half), bf16),
            pltpu.VMEM((3, 16, width), f32),
            pltpu.VMEM((3, 16, width), f32),
            dma((1,)),
            dma((8,)),
            dma((8,)),
        ],
        compiler_params=pltpu.CompilerParams(
            vmem_limit_bytes=VMEM_BYTES, collective_id=1, has_side_effects=True
        ),
    )(ga.reshape(2, 2, 2, depth, width), small2, small3, gb, qb)


def run_group(patches, counts, kept, cot, vec, qkv_b, fc1_b, wqkv, wproj, fc1, fc2, me, own):
    images, patch_count, width = patches.shape
    slot_count = cot.shape[1]
    inner = wproj.shape[1]
    pairs = inner // KEYS
    groups, unit = fc1.shape[0], fc1.shape[3]
    cap = -(-images * ROWS // BLOCK) * BLOCK
    nmax = cap // BLOCK
    dma = pltpu.SemaphoreType.DMA
    vis, gm, qkv, att, mid = pl.pallas_call(
        functools.partial(attend_kernel, images, pairs),
        name="attend",
        in_specs=[SMEM, VMEM, ANY, ANY, ANY, ANY, VMEM, VMEM],
        out_specs=[ANY] * 5,
        out_shape=[
            struct((cap, width), bf16),
            struct((cap, width), bf16),
            struct((cap, 3 * inner), bf16),
            struct((cap, inner), bf16),
            struct((cap, width), f32),
        ],
        scratch_shapes=[
            pltpu.SMEM((images,), jnp.int32),
            pltpu.VMEM((images, patch_count, width), bf16),
            pltpu.VMEM((images, ROWS, width), bf16),
            pltpu.VMEM((width, 3 * inner), bf16),
            pltpu.VMEM((width, inner), bf16),
            pltpu.VMEM((cap + KEYS, width), bf16),
            pltpu.VMEM((cap + KEYS, width), bf16),
            pltpu.VMEM((cap + KEYS, 3 * inner), bf16),
            pltpu.VMEM((cap + KEYS, inner), bf16),
            pltpu.VMEM((cap, width), f32),
            dma((images,)),
            dma((images,)),
            dma((5, nmax)),
            dma((2,)),
        ],
        **PARAMS,
    )(counts, kept, patches, cot, wqkv, wproj, vec, qkv_b)
    out, gmid, gfc, gb, small2 = pl.pallas_call(
        functools.partial(mlp_kernel, images, groups),
        name="mlp",
        in_specs=[SMEM, SMEM, ANY, ANY, ANY, ANY, VMEM, VMEM],
        out_specs=[ANY, ANY, VMEM, VMEM, VMEM],
        out_shape=[
            struct((images, slot_count, width), bf16),
            struct((cap, width), f32),
            struct((width, 2 * unit), bf16),
            struct((8, unit), f32),
            struct((3, 8, width), f32),
        ],
        scratch_shapes=[
            pltpu.SMEM((images,), jnp.int32),
            pltpu.VMEM((cap, width), f32),
            pltpu.VMEM((cap, width), bf16),
            pltpu.VMEM((cap + KEYS, width), bf16),
            pltpu.VMEM((images, slot_count, width), bf16),
            pltpu.VMEM((2, width, unit), f32),
            pltpu.VMEM(fc1.shape, bf16),
            pltpu.VMEM((groups, fc2.shape[0]) + fc2.shape[2:], bf16),
            dma((2, nmax)),
            dma((nmax,)),
            dma((images,)),
            dma((2, groups)),
        ],
        **PARAMS,
    )(me, counts, mid, gm, fc1, fc2, vec, fc1_b)
    window = -(-own // KEYS) * KEYS
    pg, ga, small3, qb = pl.pallas_call(
        functools.partial(back_kernel, images, pairs),
        name="back",
        in_specs=[SMEM, SMEM, VMEM, ANY, ANY, ANY, ANY, ANY, ANY, VMEM],
        out_specs=[ANY, VMEM, VMEM, VMEM],
        out_shape=[
            struct((patch_count, images, width), f32),
            struct((width, 4 * own), bf16),
            struct((3, 8, width), f32),
            struct((2, 8, own), f32),
        ],
        scratch_shapes=[
            pltpu.SMEM((images,), jnp.int32),
            pltpu.VMEM((3, BLOCK, width), f32),
            pltpu.VMEM((cap + KEYS, 3 * inner), bf16),
            pltpu.VMEM((cap, window), bf16),
            pltpu.VMEM((cap, width), bf16),
            pltpu.VMEM((cap + KEYS, inner), bf16),
            pltpu.VMEM((cap + KEYS, 3 * inner), bf16),
            pltpu.VMEM((width, 3 * window), f32),
            pltpu.VMEM((width, window), f32),
            pltpu.VMEM((2, 8, window), f32),
            pltpu.VMEM((4, patch_count, width), f32),
            pltpu.VMEM((width, 3 * inner), bf16),
            pltpu.VMEM((width, inner), bf16),
            dma((3, nmax)),
            dma((4,)),
            dma((2,)),
            dma((3,)),
        ],
        **PARAMS,
    )(me, counts, kept, gmid, qkv, att, vis, wqkv, wproj, vec)
    return out, pg.transpose(1, 0, 2), (gfc, ga, small2, small3, gb, qb)


def per_device(
    patches,
    counts,
    kept_patches,
    cotangent,
    norm_gains,
    shifts,
    qkv_weight,
    qkv_bias,
    proj_weight,
    fc1_weight,
    fc1_bias,
    fc2_weight,
):
    image_count, patch_count, width = patches.shape
    n_mp = lax.axis_size("mp")
    me = lax.axis_index("mp").astype(jnp.int32).reshape(1)
    own = qkv_weight.shape[2]
    inner = own * n_mp

    n_dp = lax.axis_size("dp")
    depth = width // n_dp
    direct = n_dp == 8 and n_mp == 4 and depth % 16 == 0 and image_count == 24 and patch_count % 28 == 0
    if direct:
        wqkv, wproj, fc1, fc2, patches, vec, qkv_b, fc1_b = gather_weights(
            qkv_weight.transpose(1, 0, 2), proj_weight, fc1_weight, fc2_weight.T,
            norm_gains, shifts, qkv_bias, fc1_bias.reshape(1, -1), patches, n_dp, n_mp,
        )
    else:
        vec = lax.all_gather(jnp.concatenate([norm_gains, shifts]), "dp", axis=1, tiled=True)
        vec = jnp.pad(vec.astype(f32), ((0, 2), (0, 0)))
        wqkv = lax.all_gather(lax.all_gather(qkv_weight, "mp", axis=2, tiled=True), "dp", axis=0, tiled=True)
        wqkv = wqkv.reshape(width, 3 * inner)
        qkv_b = lax.all_gather(qkv_bias, "mp", axis=1, tiled=True).astype(f32)
        wproj = lax.all_gather(lax.all_gather(proj_weight.T, "mp", axis=1, tiled=True), "dp", axis=0, tiled=True)
        both = jnp.stack([fc1_weight, fc2_weight.T])
        both = lax.all_gather(lax.all_gather(both, "mp", axis=1), "dp", axis=2, tiled=True)
        fc1 = both[0].reshape(n_mp, 1, width, width)
        fc2 = both[1].reshape(1, n_mp, width, width)
        fc1_b = lax.all_gather(fc1_bias, "mp", axis=0).astype(f32)

    group = max(n for n in range(1, GROUP_MAX + 1) if image_count % n == 0)
    outs, pgs, grads = [], [], []
    for first in range(0, image_count, group):
        part = slice(first, first + group)
        out, pg, grad = run_group(
            patches[part], counts[part], kept_patches[part], cotangent[part],
            vec, qkv_b, fc1_b, wqkv, wproj, fc1, fc2, me, own,
        )
        outs.append(out)
        pgs.append(pg)
        grads.append(grad)
    if len(grads) > 1:
        grads = [tuple(sum(item.astype(f32) for item in items) for items in zip(*grads))]
    gfc, ga, small2, small3, gb, qb = grads[0]
    hid = fc1_weight.shape[1]
    gfc = lax.psum_scatter(gfc.astype(bf16), "dp", scatter_dimension=0, tiled=True)
    if direct and len(outs) == 1:
        main, small = scatter_grads(ga.astype(bf16).reshape(n_dp, depth, -1), small2, small3, gb, qb)
        place = lax.axis_index("dp").astype(jnp.int32).reshape(1)
        g_qkv, g_proj, g_fc1, g_fc2, g_gain, g_shift, g_qb, g_fb = finish(place, main, small, gfc, n_dp)
        return (
            outs[0], pgs[0], g_gain, g_shift, g_qkv.transpose(1, 0, 2), g_qb, g_proj, g_fc1,
            g_fb.reshape(-1), g_fc2.T,
        )
    else:
        gfc = gfc.astype(f32)
        main = lax.psum_scatter(ga.astype(bf16), "dp", scatter_dimension=0, tiled=True).astype(f32)
        rows = [small3[0], small2[0], small3[2], small3[1], small2[1], small2[2], gb]
        rows += [jnp.pad(qb[n], ((0, 0), (0, width - own))) for n in range(2)]
        small = lax.psum(jnp.stack([jnp.sum(row, axis=0) for row in rows]), "dp")
    mine = lax.dynamic_slice_in_dim(small[:6], lax.axis_index("dp") * depth, depth, 1)
    return (
        outs[0] if len(outs) == 1 else jnp.concatenate(outs, axis=0),
        pgs[0] if len(pgs) == 1 else jnp.concatenate(pgs, axis=0),
        mine[:2],
        mine[2:],
        jnp.stack([main[:, j * own : (j + 1) * own] for j in range(3)]).transpose(1, 0, 2),
        small[7:9, :own],
        main[:, 3 * own : 4 * own].T,
        gfc[:, :hid],
        small[6],
        gfc[:, hid:].T,
    )


def solution(mesh):
    placed = (
        P("dp", None, None),
        P("dp"),
        P("dp", None),
        P("dp", None, None),
        P(None, "dp"),
        P(None, "dp"),
        P("dp", None, "mp"),
        P(None, "mp"),
        P("mp", "dp"),
        P("dp", "mp"),
        P("mp"),
        P("mp", "dp"),
    )
    return jax.shard_map(
        per_device,
        mesh=mesh,
        in_specs=placed,
        out_specs=(
            P("dp", None, None),
            P("dp", None, None),
            P(None, "dp"),
            P(None, "dp"),
            P("dp", None, "mp"),
            P(None, "mp"),
            P("mp", "dp"),
            P("dp", "mp"),
            P("mp"),
            P("mp", "dp"),
        ),
        check_vma=False,
    )
```
